128 devices in a mesh: section: 2 (over core), dp: 16 (over y, x), tensor: 4 (over z).
Axes of the slice: x: 4, y: 4, z: 4, core: 2. Of those that a mesh axis runs over, the one named last changes fastest.
Arguments:
- layer_input: bfloat16 [2, 4096, 2, 4096], P('section', 'dp', None, 'tensor'), may hold values from -60 to 60
- norm_gain: float32 [2, 4096], P('section'), may hold values from 0.5 to 1.5
- upstream_grad: bfloat16 [2, 4096, 2, 4096], P('section', 'dp', None, 'tensor'), may hold values from -80 to 80
- saved_queries: bfloat16 [2, 4096, 2, 2048], P('section', 'dp', None, 'tensor'), may hold values from -150 to 150
- saved_keys: bfloat16 [2, 4096, 2, 1024], P('section', 'dp', None, 'tensor'), may hold values from -5 to 5
- saved_values: bfloat16 [2, 4096, 2, 1024], P('section', 'dp', None, 'tensor'), may hold values from -6 to 6
- segment_ids: int32 [2, 2, 4096], P('section', None, 'dp'), may hold values from 0 to 63, never falling along the last dimension, each value on 1 to 128 neighbouring positions
- batch_order: int32 [2, 16, 2], P('section', 'dp'), may hold values from 0 to 1, each once within a row
- qkv_weight: bfloat16 [2, 4096, 4096], P('section', None, 'tensor'), may hold values from -0.09375 to 0.09375
- out_weight: bfloat16 [2, 2048, 4096], P('section', 'tensor'), may hold values from -0.125 to 0.125
Outputs:
- passed_grad: bfloat16 [2, 4096, 2, 4096], P('section', 'dp', None, 'tensor')
- qkv_grad: float32 [2, 4096, 4096], P('section', 'dp', 'tensor')
- out_grad: float32 [2, 2048, 4096], P('section', 'tensor', 'dp')
- gain_grad: float32 [2, 4096], P('section', 'tensor')
The draws below stay inside these ranges and needn't reach their ends.
All inputs are finite; a program needn't handle non-finite values.
Results may differ from the reference program's by a relative error of at most 0.0058.
The reference program's roundings to bfloat16 on the way count: a program that leaves them out, or rounds other values in their place, can miss the bound.
Values may be sent and summed in bfloat16 or wider, within the bound.
A program may use at most 192 MiB of HBM per device.

```python
import math
import jax
import jax.numpy as jnp
import numpy as np
from jax import lax

D = 4096
HD = 128
KV = 8
HEADS = 16
SEQ = 256
MICRO = 2
SECTIONS = 2
TOKENS = 4096
N_DP = 16


def draw_layer_input(key, part):
    shape_full = (SECTIONS, TOKENS, MICRO, D)
    noise_base = jnp.clip(jax.random.normal(jax.random.fold_in(key, 1), shape_full, jnp.float32), -6.0, 6.0)
    row_scale = jnp.exp(jax.random.uniform(jax.random.fold_in(key, 2), (SECTIONS, TOKENS, MICRO, 1), jnp.float32, math.log(0.3), math.log(3.0)))
    column_scale = jnp.exp(jax.random.uniform(jax.random.fold_in(key, 3), (1, 1, 1, D), jnp.float32, 0.0, math.log(10.0)))
    return (noise_base * row_scale * column_scale / 3.0).astype(jnp.bfloat16)


def draw_upstream_grad(key, part):
    shape_full = (SECTIONS, TOKENS, MICRO, D)
    noise_base = jnp.clip(jax.random.normal(jax.random.fold_in(key, 21), shape_full, jnp.float32), -6.0, 6.0)
    token_ramp = 1.0 + 2.0 * jnp.arange(TOKENS, dtype=jnp.float32) / (TOKENS - 1)
    return (noise_base * token_ramp[None, :, None, None]).astype(jnp.bfloat16)


def query_key(key):
    key_vals = jnp.clip(jax.random.normal(jax.random.fold_in(key, 11), (SECTIONS, TOKENS, MICRO, KV, HD), jnp.float32), -5.0, 5.0)
    query_vals = jnp.clip(jax.random.normal(jax.random.fold_in(key, 12), (SECTIONS, TOKENS, MICRO, KV, HEADS // KV, HD), jnp.float32), -5.0, 5.0)
    return (query_vals.reshape(SECTIONS, TOKENS, MICRO, HEADS * HD), key_vals.reshape(SECTIONS, TOKENS, MICRO, KV * HD))


def draw_saved_queries(key, part):
    return query_key(key)[0].astype(jnp.bfloat16)


def draw_saved_keys(key, part):
    return query_key(key)[1].astype(jnp.bfloat16)


def block_levels(rng, shape, split, low, top_value):
    gain = 1.0
    for position, parts in split:
        draws = jax.random.uniform(jax.random.fold_in(jax.random.fold_in(rng, 6), position), (parts,), jnp.float32, low / len(split), top_value / len(split))
        gain = gain * jnp.repeat(jnp.exp(draws), shape[position] // parts).reshape((-1,) + (1,) * (len(shape) - 1 - position))
    return gain


def profile(count, total, reach, slope):
    loads = [(1 << 20) // math.isqrt(standing ** slope) + 1 for standing in range(2, count + 1)]
    spare, holding = total - reach - (count - 1), [1] * (count - 1)
    while spare > 0:
        free = [i for i in range(count - 1) if holding[i] < reach]
        mass, budget = sum([loads[i] for i in free]), spare
        for i in free:
            extra = min(reach - holding[i], max(1, budget * loads[i] // mass), spare)
            holding[i] = holding[i] + extra
            spare = spare - extra
    return np.array([reach] + holding)


def uneven(key, amount, total, reach, skew):
    if amount == 2:
        one = jax.random.randint(key, (), max(1, total - reach), min(reach, total - 1) + 1)
        return jnp.stack([one, total - one])
    sizes = jnp.asarray(profile(amount, total, reach, skew), jnp.int32)
    pairs = (amount - 1) // 2
    donor, sink = sizes[1:1 + 2 * pairs:2], sizes[2:2 + 2 * pairs:2]
    room = jnp.minimum(donor - 1, reach - sink)
    moved = jax.random.randint(jax.random.fold_in(key, 1), (pairs,), 0, 1 << 20) % (room + 1)
    sizes = sizes.at[1:1 + 2 * pairs:2].set(donor - moved).at[2:2 + 2 * pairs:2].set(sink + moved)
    return sizes[jax.random.permutation(jax.random.fold_in(key, 2), amount)]


def gaussian(own_key, shape, scale, most, cuts=(), kind=jnp.bfloat16):
    drawn = jax.random.normal(own_key, shape, jnp.float32) * scale
    if len(cuts) > 0:
        drawn = block_levels(own_key, shape, cuts, -0.22, 0.18) * drawn
    return jnp.clip(drawn, min=-most, max=most).astype(kind)


def setup_inputs(seed: int = 0) -> dict:
    arg_keys = jax.random.split(jax.random.key(seed), 11)
    layer_input = draw_layer_input(jax.random.fold_in(arg_keys[10], 71), 0)
    norm_gain = jnp.clip(1.0 + 0.1 * jax.random.normal(arg_keys[1], (SECTIONS, D), jnp.float32), 0.5, 1.5)
    upstream_grad = draw_upstream_grad(jax.random.fold_in(arg_keys[10], 71), 0)
    saved_queries = draw_saved_queries(jax.random.fold_in(arg_keys[10], 71), 0)
    saved_keys = draw_saved_keys(jax.random.fold_in(arg_keys[10], 71), 0)
    saved_values = gaussian(arg_keys[5], (SECTIONS, TOKENS, MICRO, KV * HD), 1.0, 6.0, ((0, 2), (1, 16), (3, 4)))
    segment_ids = jax.vmap(lambda own: jnp.searchsorted(jnp.cumsum(uneven(own, 4 * N_DP, TOKENS, SEQ // 2, 1)), jnp.arange(TOKENS), side="right"))(jax.random.split(arg_keys[6], SECTIONS * MICRO)).reshape((SECTIONS, MICRO, TOKENS)).astype(jnp.int32)
    batch_order = jax.vmap(lambda own: jax.random.permutation(own, MICRO))(jax.random.split(arg_keys[7], SECTIONS * N_DP)).reshape((SECTIONS, N_DP, MICRO)).astype(jnp.int32)
    qkv_weight = gaussian(arg_keys[8], (SECTIONS, D, (HEADS + 2 * KV) * HD), D ** -0.5, 0.09375, ((0, 2), (2, 4)))
    out_weight = gaussian(arg_keys[9], (SECTIONS, HEADS * HD, D), (HEADS * HD) ** -0.5, 0.125, ((0, 2), (1, 4)))
    return dict(layer_input=layer_input, norm_gain=norm_gain, upstream_grad=upstream_grad, saved_queries=saved_queries, saved_keys=saved_keys, saved_values=saved_values, segment_ids=segment_ids, batch_order=batch_order, qkv_weight=qkv_weight, out_weight=out_weight)


EPS = 1e-05

def attention_back(queries, saved_keys, saved_values, visible, attn_grad):
    score_scale = 1.0 / math.sqrt(HD)
    query_f32 = queries.astype(jnp.float32)
    key_f32 = saved_keys.astype(jnp.float32)
    value_f32 = saved_values.astype(jnp.float32)
    grad_f32 = attn_grad.astype(jnp.float32)
    visible_full = visible[:, :, None, None, :, :]
    scores = jnp.einsum('rimkgh,rjmkh->rmkgij', query_f32, key_f32) * score_scale
    scores = jnp.where(visible_full, scores, -1e+30)
    row_max = lax.optimization_barrier(jnp.max(scores, axis=-1, keepdims=True))
    exp_scores = jnp.where(visible_full, jnp.exp(scores - row_max), 0.0)
    attn_probs = exp_scores / lax.optimization_barrier(jnp.sum(exp_scores, axis=-1, keepdims=True))
    probs_bf16 = lax.optimization_barrier(attn_probs.astype(jnp.bfloat16)).astype(jnp.float32)
    attn_out = jnp.einsum('rmkgij,rjmkh->rimkgh', probs_bf16, value_f32).astype(jnp.bfloat16)
    probs_grad = jnp.einsum('rimkgh,rjmkh->rmkgij', grad_f32, value_f32)
    row_dot = lax.optimization_barrier(jnp.sum(attn_probs * probs_grad, axis=-1, keepdims=True))
    score_grad = (attn_probs * (probs_grad - row_dot) * score_scale).astype(jnp.bfloat16)
    score_grad = lax.optimization_barrier(score_grad).astype(jnp.float32)
    query_grad = jnp.einsum('rmkgij,rjmkh->rimkgh', score_grad, key_f32)
    key_grad = jnp.einsum('rmkgij,rimkgh->rjmkh', score_grad, query_f32)
    value_grad = jnp.einsum('rmkgij,rimkgh->rjmkh', probs_bf16, grad_f32)
    qkv_grads = jnp.concatenate([query_grad, key_grad[..., None, :], value_grad[..., None, :]], axis=-2)
    return (attn_out, qkv_grads.astype(jnp.bfloat16))

def layer_back(layer_input, gain_vec, upstream, queries, saved_keys, saved_values, segment_rows, qkv_weight, out_weight):
    widened = layer_input.astype(jnp.float32)
    root_mean = jnp.sqrt(lax.optimization_barrier(jnp.mean(widened * widened, axis=-1, keepdims=True)) + EPS)
    unit_rows = widened / root_mean
    normed = lax.optimization_barrier((unit_rows * gain_vec).astype(jnp.bfloat16)).astype(jnp.float32)
    upstream_f32 = upstream.astype(jnp.float32)
    attn_grad = jnp.einsum('tmd,cd->tmc', upstream_f32, out_weight.astype(jnp.float32)).astype(jnp.bfloat16)
    attn_grad = lax.optimization_barrier(attn_grad)
    group_size = HEADS // KV
    query_shape = (N_DP, SEQ, MICRO, KV, group_size, HD)
    value_shape = (N_DP, SEQ, MICRO, KV, HD)
    segment_blocks = segment_rows.reshape(MICRO, N_DP, SEQ).transpose(1, 0, 2)
    positions = jnp.arange(SEQ)
    causal = positions[None, :] <= positions[:, None]
    visible = (segment_blocks[:, :, :, None] == segment_blocks[:, :, None, :]) & causal[None, None]
    attn_out, qkv_grads = attention_back(queries.reshape(query_shape), saved_keys.reshape(value_shape), saved_values.reshape(value_shape), visible, attn_grad.reshape(query_shape))
    attn_out = lax.optimization_barrier(attn_out).reshape(TOKENS, MICRO, HEADS * HD).astype(jnp.float32)
    qkv_grads = lax.optimization_barrier(qkv_grads).reshape(TOKENS, MICRO, (HEADS + 2 * KV) * HD).astype(jnp.float32)
    out_grad = jnp.einsum('tmc,tmd->cd', attn_out, upstream_f32) / N_DP
    qkv_grad = jnp.einsum('tmd,tmc->dc', normed, qkv_grads) / N_DP
    normed_grad = jnp.einsum('tmc,dc->tmd', qkv_grads, qkv_weight.astype(jnp.float32))
    gain_grad = lax.optimization_barrier(jnp.sum(normed_grad * unit_rows, axis=(0, 1))) / N_DP
    scaled = normed_grad * gain_vec
    through = upstream_f32 + (scaled - unit_rows * lax.optimization_barrier(jnp.mean(scaled * unit_rows, axis=-1, keepdims=True))) / root_mean
    return (through.astype(jnp.bfloat16), qkv_grad, out_grad, gain_grad)

def reorder(through, order_rows):
    blocks = through.reshape(N_DP, SEQ, MICRO, D)
    index_rows = order_rows.astype(jnp.int32)[:, None, :, None]
    picked = jnp.take_along_axis(blocks, index_rows, axis=2)
    return picked.reshape(TOKENS, MICRO, D)

def reference(layer_input, norm_gain, upstream_grad, saved_queries, saved_keys, saved_values, segment_ids, batch_order, qkv_weight, out_weight):
    sent_list = []
    qkv_list = []
    out_list = []
    gain_list = []
    for phase_index in range(SECTIONS):
        through, qkv_grad, out_grad, gain_grad = layer_back(layer_input[phase_index], norm_gain[phase_index], upstream_grad[phase_index], saved_queries[phase_index], saved_keys[phase_index], saved_values[phase_index], segment_ids[phase_index], qkv_weight[phase_index], out_weight[phase_index])
        sent_list.append(reorder(through, batch_order[phase_index]))
        qkv_list.append(qkv_grad)
        out_list.append(out_grad)
        gain_list.append(gain_grad)
    passed_grad = jnp.stack(sent_list[1:] + [jnp.zeros_like(sent_list[0])])
    return (passed_grad, jnp.stack(qkv_list), jnp.stack(out_list), jnp.stack(gain_list))
```

```python
import math

import jax
import jax.numpy as jnp
from jax import lax
from jax.experimental import pallas as pl
from jax.experimental.pallas import tpu as pltpu
from jax.sharding import PartitionSpec as P

HD = 128
EPS = 1e-05
MESH = pl.DeviceIdType.MESH
F32 = jnp.float32
BF16 = jnp.bfloat16
SCALE = 1.0 / math.sqrt(HD)

NT = (((1,), (1,)), ((), ()))
NN = (((1,), (0,)), ((), ()))
TN = (((0,), (0,)), ((), ()))


def dot(a, b, dims):
    return lax.dot_general(a, b, dims, preferred_element_type=F32)


def rows_of(index, size):
    return pl.ds(pl.multiple_of(index * size, size), size)


def as_row(column):
    return jnp.broadcast_to(column, (256, 128)).T[0:8, :]


def as_column(row):
    return jnp.broadcast_to(row, (128, 256)).T


def kernel(
    up, inp, q, k, v, seg, gain, order, wq_hbm, wo_hbm,
    passed, qg, og, gg,
    upb, nm, wo, wq, probs, ao, aga, ag, qk,
    o_s, o_y1, o_y2, o_x, o_x1, o_x2,
    q_s, q_x1, q_x2, q_y, q_y1, q_y2,
    g_1, g_2, ssq, rowp, root, rtot, segc, gp, gz, gx, gy,
    lsem, ssem, rsem,
):
    sec = lax.axis_index("section")
    dp = lax.axis_index("dp")
    z = lax.axis_index("tensor")
    y = lax.div(dp, 4)
    x = lax.rem(dp, 4)

    z_to = [{"tensor": lax.rem(z + s, 4)} for s in range(4)]
    x_to = [{"dp": y * 4 + lax.rem(x + s, 4)} for s in range(4)]
    y_to = [{"dp": lax.rem(y + s, 4) * 4 + x} for s in range(4)]
    other = {"section": 1 - sec}

    counter = [0]
    sent = []

    def copy(src, dst, to, keep=True):
        index = counter[0]
        counter[0] += 1
        made = pltpu.make_async_remote_copy(
            src_ref=src,
            dst_ref=dst,
            send_sem=ssem.at[index],
            recv_sem=rsem.at[index],
            device_id=to,
            device_id_type=MESH,
        )
        if keep:
            sent.append(made)
        return made

    loads = [
        pltpu.make_async_copy(wo_hbm.at[:, pl.ds(1024 * b, 1024)], wo.at[b], lsem.at[b])
        for b in range(4)
    ]
    loads.append(pltpu.make_async_copy(wq_hbm, wq, lsem.at[4]))
    for one in loads:
        one.start()

    barrier = pltpu.get_barrier_semaphore()
    peers = z_to[1:] + x_to[1:] + y_to[1:] + [other]
    for peer in peers:
        pl.semaphore_signal(barrier, inc=1, device_id=peer, device_id_type=MESH)
    pl.semaphore_wait(barrier, len(peers))

    first, second = pl.ds(0, 256), pl.ds(256, 256)

    def gather_start(own, slots):
        made = {
            "ra": copy(own.at[first], slots[1].at[first], z_to[1]),
            "lb": copy(own.at[second], slots[2].at[second], z_to[3]),
            "rb": copy(own.at[second], slots[1].at[second], z_to[1]),
            "la": copy(own.at[first], slots[2].at[first], z_to[3]),
        }
        for name in ("ra", "lb", "rb", "la"):
            made[name].start()
        return made

    def gather_relay(made, slots):
        made["ra"].wait_recv()
        made["fa"] = copy(slots[1].at[first], slots[3].at[first], z_to[1])
        made["fa"].start()
        made["lb"].wait_recv()
        made["fb"] = copy(slots[2].at[second], slots[3].at[second], z_to[3])
        made["fb"].start()

    def add_rows(dst, src, count, step=32):
        @pl.loop(0, count // step)
        def _(i):
            part = rows_of(i, step)
            dst[part, :] = (dst[part, :].astype(F32) + src[part, :].astype(F32)).astype(BF16)

    def scatter(far, right, left, half, land, full, to, keep=True):
        return {
            "a": copy(far.at[pl.ds(0, half)], land.at[0], to[1], keep),
            "b": copy(far.at[pl.ds(half, half)], land.at[1], to[3], keep),
            "r": copy(right, full.at[0], to[1], keep),
            "l": copy(left, full.at[1], to[3], keep),
            "add_a": (right.at[pl.ds(0, half)], land.at[0], half),
            "add_b": (left.at[pl.ds(half, half)], land.at[1], half),
        }

    def scatter_start(made):
        made["a"].start()
        made["b"].start()

    def scatter_mid(made):
        made["a"].wait_recv()
        add_rows(*made["add_a"])
        made["r"].start()
        made["b"].wait_recv()
        add_rows(*made["add_b"])
        made["l"].start()

    def scatter_wait(made):
        made["r"].wait_recv()
        made["l"].wait_recv()

    up_slots = [up, upb.at[0], upb.at[1], upb.at[2]]
    nm_slots = [nm.at[0], nm.at[1], nm.at[2], nm.at[3]]
    offsets = (0, 3, 1, 2)

    up_made = gather_start(up, up_slots)

    for m in range(2):
        total = jnp.zeros((256, 1), F32)
        for c in range(4):
            wide = inp[pl.ds(256 * m, 256), pl.ds(256 * c, 256)].astype(F32)
            total += jnp.sum(wide * wide, axis=-1, keepdims=True)
        ssq[0, :, pl.ds(256 * m, 256)] = as_row(total)
    ssq_made = [copy(ssq.at[0], ssq.at[s], z_to[s]) for s in (1, 2, 3)]
    for one in ssq_made:
        one.start()

    for m in range(2):
        ids = seg[pl.ds(m, 1), :].astype(F32)
        segc[pl.ds(256 * m, 256), :] = jnp.broadcast_to(ids, (256, 256)).T

    @pl.loop(0, 8)
    def _(i):
        m = lax.div(i, 4)
        head = lax.rem(i, 4)
        rows = rows_of(m, 256)
        lanes = rows_of(lax.div(head, 2), 128)
        scores = dot(q[rows, rows_of(head, 128)], k[rows, lanes], NT) * SCALE
        low = lax.broadcasted_iota(jnp.int32, (256, 256), 0)
        high = lax.broadcasted_iota(jnp.int32, (256, 256), 1)
        ids = seg[pl.ds(m, 1), :].astype(F32)
        visible = (segc[rows, :] == ids) & (high <= low)
        scores = jnp.where(visible, scores, -1e30)
        top = jnp.max(scores, axis=-1, keepdims=True)
        shifted = jnp.where(visible, jnp.exp(scores - top), 0.0)
        weights = shifted / jnp.sum(shifted, axis=-1, keepdims=True)
        probs[i] = weights
        ao[rows, rows_of(head, 128)] = dot(weights.astype(BF16), v[rows, lanes], NN).astype(BF16)

    for one in loads[:4]:
        one.wait()

    def take_upstream(slot):
        block = lax.rem(z + offsets[slot], 4)
        ref = up_slots[slot]

        @pl.loop(0, 2)
        def _(m):
            rows = rows_of(m, 256)
            term = dot(ref[rows, :], wo[block], NT)
            if slot == 0:
                aga[rows, :] = term
            else:
                aga[rows, :] += term

    def out_terms(slot):
        block = lax.rem(z + offsets[slot], 4)
        ref = up_slots[slot]

        @pl.loop(0, 4)
        def _(j):
            lanes = rows_of(j, 256)
            o_s[block, :, lanes] = dot(ao[...], ref[:, lanes], TN).astype(BF16)

    take_upstream(0)
    out_terms(0)
    gather_relay(up_made, up_slots)

    for one in ssq_made:
        one.wait_recv()
    gain_own = gain[:, pl.ds(pl.multiple_of(z * 1024, 1024), 1024)]
    for m in range(2):
        lanes = pl.ds(256 * m, 256)
        total = ssq[0, :, lanes] + ssq[1, :, lanes] + ssq[2, :, lanes] + ssq[3, :, lanes]
        root[lanes, :] = as_column(jnp.sqrt(total * (1.0 / 4096) + EPS)[0:1, :])

    @pl.loop(0, 16)
    def _(i):
        rows = rows_of(i, 32)
        unit = inp[rows, :].astype(F32) / root[rows, 0:1]
        nm[0, rows, :] = (unit * gain_own).astype(BF16)

    nm_made = gather_start(nm.at[0], nm_slots)

    up_made["rb"].wait_recv()
    take_upstream(1)
    out_terms(1)
    up_made["la"].wait_recv()
    take_upstream(2)
    out_terms(2)
    up_made["fa"].wait_recv()
    up_made["fb"].wait_recv()
    take_upstream(3)

    @pl.loop(0, 16)
    def _(i):
        rows = rows_of(i, 32)
        ag[rows, :] = aga[rows, :].astype(BF16)

    @pl.loop(0, 4)
    def _(i):
        m = lax.div(i, 2)
        group = lax.rem(i, 2)
        rows = rows_of(m, 256)
        lanes = rows_of(group, 128)
        key_grad = jnp.zeros((256, 128), F32)
        value_grad = jnp.zeros((256, 128), F32)
        for h in range(2):
            head = rows_of(group * 2 + h, 128)
            grad = ag[rows, head]
            weights = probs[i * 2 + h]
            probs_grad = dot(grad, v[rows, lanes], NT)
            row_dot = jnp.sum(weights * probs_grad, axis=-1, keepdims=True)
            score_grad = (weights * (probs_grad - row_dot) * SCALE).astype(BF16)
            at = rows_of(group * 4 + h, 128)
            qk[rows, at] = dot(score_grad, k[rows, lanes], NN).astype(BF16)
            key_grad += dot(score_grad, q[rows, head], TN)
            value_grad += dot(weights.astype(BF16), grad, TN)
        qk[rows, rows_of(group * 4 + 2, 128)] = key_grad.astype(BF16)
        qk[rows, rows_of(group * 4 + 3, 128)] = value_grad.astype(BF16)

    loads[4].wait()

    q_made = {}

    def qkv_terms(slot):
        block = lax.rem(z + offsets[slot], 4)

        @pl.loop(0, 4)
        def _(j):
            target = lax.rem(x + j, 4)
            lanes = rows_of(target, 256)
            term = dot(nm[slot, :, lanes], qk[...], TN)
            weighted = jnp.sum(term * wq[block, lanes, :].astype(F32), axis=-1, keepdims=True)
            gp[slot, :, lanes] = as_row(weighted)
            q_s[slot, j] = term.astype(BF16)

        q_made[slot] = scatter(
            q_s.at[slot, 2], q_s.at[slot, 1], q_s.at[slot, 3], 128, q_x1.at[slot], q_x2.at[slot], x_to
        )
        scatter_start(q_made[slot])

    def qkv_mid(slot):
        scatter_mid(q_made[slot])

    def qkv_end(slot):
        block = lax.rem(z + offsets[slot], 4)
        scatter_wait(q_made[slot])

        @pl.loop(0, 8)
        def _(i):
            rows = rows_of(i, 32)
            total = (
                q_s[slot, 0, rows, :].astype(F32)
                + q_x2[slot, 0, rows, :].astype(F32)
                + q_x2[slot, 1, rows, :].astype(F32)
            )
            q_y[block, rows, :] = total.astype(BF16)

    qkv_terms(0)
    out_terms(3)
    o_made = scatter(
        o_s.at[lax.rem(y + 2, 4)], o_s.at[lax.rem(y + 1, 4)], o_s.at[lax.rem(y + 3, 4)],
        256, o_y1, o_y2, y_to,
    )
    scatter_start(o_made)
    gather_relay(nm_made, nm_slots)
    qkv_mid(0)

    z_made = scatter(wo.at[2], wo.at[1], wo.at[3], 256, g_1, g_2, z_to, keep=False)

    @pl.when(sec == 1)
    def _():
        @pl.loop(0, 16)
        def _(i):
            j = lax.div(i, 4)
            part = rows_of(lax.rem(i, 4), 256)
            term = dot(qk[...], wq[lax.rem(z + j, 4), part, :], NT)
            wo[j, :, part] = term.astype(BF16)

        scatter_start(z_made)

    nm_made["rb"].wait_recv()
    qkv_terms(1)
    nm_made["la"].wait_recv()
    qkv_terms(2)
    scatter_mid(o_made)
    qkv_mid(1)
    qkv_mid(2)
    nm_made["fa"].wait_recv()
    nm_made["fb"].wait_recv()
    qkv_terms(3)

    gz_made = [
        copy(gp.at[slot], gz.at[slot - 1], z_to[offsets[slot]]) for slot in (1, 2, 3)
    ]
    for one in gz_made:
        one.start()
    qkv_end(0)

    scatter_wait(o_made)
    o_own = o_s.at[y]

    @pl.loop(0, 4)
    def _(j):
        lanes = rows_of(lax.rem(x + j, 4), 256)

        @pl.loop(0, 8)
        def _(i):
            rows = rows_of(i, 64)
            total = (
                o_own[rows, lanes].astype(F32)
                + o_y2[0, rows, lanes].astype(F32)
                + o_y2[1, rows, lanes].astype(F32)
            )
            o_x[j, rows, :] = total.astype(BF16)

    ox_made = scatter(o_x.at[2], o_x.at[1], o_x.at[3], 256, o_x1, o_x2, x_to)
    scatter_start(ox_made)

    for one in gz_made:
        one.wait_recv()
    gx[0] = gp[0] + gz[0] + gz[1] + gz[2]
    gx_made = [copy(gx.at[0], gx.at[s], x_to[s]) for s in (1, 2, 3)]
    for one in gx_made:
        one.start()

    qkv_mid(3)

    @pl.when(sec == 1)
    def _():
        scatter_mid(z_made)

    scatter_mid(ox_made)
    qkv_end(1)
    qkv_end(2)

    for one in gx_made:
        one.wait_recv()
    gy[0] = gx[0] + gx[1] + gx[2] + gx[3]
    gy_made = [copy(gy.at[0], gy.at[s], y_to[s]) for s in (1, 2, 3)]
    for one in gy_made:
        one.start()

    qkv_end(3)
    qy_made = scatter(
        q_y.at[lax.rem(y + 2, 4)], q_y.at[lax.rem(y + 1, 4)], q_y.at[lax.rem(y + 3, 4)],
        128, q_y1, q_y2, y_to,
    )
    scatter_start(qy_made)

    layer = upb.at[2]
    row_made = [copy(rowp.at[0], rowp.at[s], z_to[s], keep=False) for s in (1, 2, 3)]

    def scaled_unit(rows):
        grad = (
            wo[0, rows, :].astype(F32) + g_2[0, rows, :].astype(F32) + g_2[1, rows, :].astype(F32)
        )
        return grad * gain_own, inp[rows, :].astype(F32) / root[rows, 0:1]

    @pl.when(sec == 1)
    def _():
        scatter_wait(z_made)

        @pl.loop(0, 16)
        def _(i):
            rows = rows_of(i, 32)
            scaled, unit = scaled_unit(rows)
            part = jnp.sum(scaled * unit, axis=-1, keepdims=True)
            rtot[rows, :] = jnp.broadcast_to(part, (32, 128))

        for m in range(2):
            lanes = pl.ds(256 * m, 256)
            rowp[0, :, lanes] = rtot[lanes, :].T[0:8, :]
        for one in row_made:
            one.start()

    scatter_mid(qy_made)

    passed_made = copy(layer, passed, other, keep=False)

    @pl.when(sec == 1)
    def _():
        for one in row_made:
            one.wait_recv()
        for m in range(2):
            lanes = pl.ds(256 * m, 256)
            total = rowp[0, :, lanes] + rowp[1, :, lanes] + rowp[2, :, lanes] + rowp[3, :, lanes]
            rtot[lanes, :] = as_column((total * (1.0 / 4096))[0:1, :])
        straight = order[0:1, 0:1] == 0.0

        @pl.loop(0, 16)
        def _(i):
            both = []
            for m in range(2):
                rows = pl.ds(pl.multiple_of(m * 256 + i * 16, 16), 16)
                scaled, unit = scaled_unit(rows)
                through = up[rows, :].astype(F32) + (scaled - unit * rtot[rows, 0:1]) / root[rows, 0:1]
                both.append(through)
            low, high = both
            keep_order = jnp.broadcast_to(straight, (16, 1024))
            rows = pl.ds(pl.multiple_of(i * 16, 16), 16)
            layer[rows, :] = jnp.where(keep_order, low, high).astype(BF16)
            rows = pl.ds(pl.multiple_of(256 + i * 16, 16), 16)
            layer[rows, :] = jnp.where(keep_order, high, low).astype(BF16)

        passed_made.start()

        @pl.loop(0, 16)
        def _(i):
            passed[rows_of(i, 32), :] = jnp.zeros((32, 1024), BF16)

    scatter_wait(ox_made)

    @pl.loop(0, 8)
    def _(i):
        rows = rows_of(i, 64)
        total = o_x[0, rows, :].astype(F32) + o_x2[0, rows, :].astype(F32) + o_x2[1, rows, :].astype(F32)
        og[rows, :] = total * (1.0 / 16)

    for one in gy_made:
        one.wait_recv()
    gg[...] = (gy[0] + gy[1] + gy[2] + gy[3]) / (gain_own * 16.0)

    scatter_wait(qy_made)

    @pl.loop(0, 8)
    def _(i):
        rows = rows_of(i, 32)
        total = q_y[y, rows, :].astype(F32) + q_y2[0, rows, :].astype(F32) + q_y2[1, rows, :].astype(F32)
        qg[rows, :] = total * (1.0 / 16)

    @pl.when(sec == 0)
    def _():
        passed_made.wait_recv()

    @pl.when(sec == 1)
    def _():
        for one in [z_made[name] for name in "abrl"] + row_made + [passed_made]:
            one.wait_send()

    for one in sent:
        one.wait_send()


def shards(
    layer_input,
    norm_gain,
    upstream_grad,
    saved_queries,
    saved_keys,
    saved_values,
    segment_ids,
    batch_order,
    qkv_weight,
    out_weight,
):
    def by_micro(array):
        return array[0].transpose(1, 0, 2).reshape(512, array.shape[3])

    order = jnp.broadcast_to(batch_order[0].astype(F32)[:, 0:1], (8, 128))
    vmem = pl.BlockSpec(memory_space=pltpu.VMEM)
    hbm = pl.BlockSpec(memory_space=pl.ANY)
    passed, qkv_grad, out_grad, gain_grad = pl.pallas_call(
        kernel,
        out_shape=(
            jax.ShapeDtypeStruct((512, 1024), BF16),
            jax.ShapeDtypeStruct((256, 1024), F32),
            jax.ShapeDtypeStruct((512, 256), F32),
            jax.ShapeDtypeStruct((8, 1024), F32),
        ),
        in_specs=[vmem] * 8 + [hbm] * 2,
        out_specs=(vmem,) * 4,
        scratch_shapes=[
            pltpu.VMEM((3, 512, 1024), BF16),
            pltpu.VMEM((4, 512, 1024), BF16),
            pltpu.VMEM((4, 512, 1024), BF16),
            pltpu.VMEM((4, 1024, 1024), BF16),
            pltpu.VMEM((8, 256, 256), F32),
            pltpu.VMEM((512, 512), BF16),
            pltpu.VMEM((512, 512), F32),
            pltpu.VMEM((512, 512), BF16),
            pltpu.VMEM((512, 1024), BF16),
            pltpu.VMEM((4, 512, 1024), BF16),
            pltpu.VMEM((2, 256, 1024), BF16),
            pltpu.VMEM((2, 512, 1024), BF16),
            pltpu.VMEM((4, 512, 256), BF16),
            pltpu.VMEM((2, 256, 256), BF16),
            pltpu.VMEM((2, 512, 256), BF16),
            pltpu.VMEM((4, 4, 256, 1024), BF16),
            pltpu.VMEM((4, 2, 128, 1024), BF16),
            pltpu.VMEM((4, 2, 256, 1024), BF16),
            pltpu.VMEM((4, 256, 1024), BF16),
            pltpu.VMEM((2, 128, 1024), BF16),
            pltpu.VMEM((2, 256, 1024), BF16),
            pltpu.VMEM((2, 256, 1024), BF16),
            pltpu.VMEM((2, 512, 1024), BF16),
            pltpu.VMEM((4, 8, 512), F32),
            pltpu.VMEM((4, 8, 512), F32),
            pltpu.VMEM((512, 128), F32),
            pltpu.VMEM((512, 128), F32),
            pltpu.VMEM((512, 256), F32),
            pltpu.VMEM((4, 8, 1024), F32),
            pltpu.VMEM((3, 8, 1024), F32),
            pltpu.VMEM((4, 8, 1024), F32),
            pltpu.VMEM((4, 8, 1024), F32),
            pltpu.SemaphoreType.DMA((5,)),
            pltpu.SemaphoreType.DMA((80,)),
            pltpu.SemaphoreType.DMA((80,)),
        ],
        compiler_params=pltpu.CompilerParams(
            collective_id=0, has_side_effects=True, vmem_limit_bytes=67043328
        ),
    )(
        by_micro(upstream_grad),
        by_micro(layer_input),
        by_micro(saved_queries),
        by_micro(saved_keys),
        by_micro(saved_values),
        segment_ids[0],
        norm_gain,
        order,
        qkv_weight[0].reshape(4, 1024, 1024),
        out_weight[0],
    )
    passed = passed.reshape(2, 256, 1024).transpose(1, 0, 2)
    return (passed[None], qkv_grad[None], out_grad[None], gain_grad[0:1])


def solution(mesh):
    placed = (
        P("section", "dp", None, "tensor"),
        P("section", None),
        P("section", "dp", None, "tensor"),
        P("section", "dp", None, "tensor"),
        P("section", "dp", None, "tensor"),
        P("section", "dp", None, "tensor"),
        P("section", None, "dp"),
        P("section", "dp", None),
        P("section", None, "tensor"),
        P("section", "tensor", None),
    )
    return jax.shard_map(
        shards,
        mesh=mesh,
        in_specs=placed,
        out_specs=(
            P("section", "dp", None, "tensor"),
            P("section", "dp", "tensor"),
            P("section", "tensor", "dp"),
            P("section", "tensor"),
        ),
        check_vma=False,
    )
```

```python
import math

import jax
import jax.numpy as jnp
from jax import lax
from jax.experimental import pallas as pl
from jax.experimental.pallas import tpu as pltpu
from jax.sharding import PartitionSpec as P

HD = 128
EPS = 1e-05
MESH = pl.DeviceIdType.MESH
F32 = jnp.float32
BF16 = jnp.bfloat16
SCALE = 1.0 / math.sqrt(HD)

NT = (((1,), (1,)), ((), ()))
NN = (((1,), (0,)), ((), ()))
TN = (((0,), (0,)), ((), ()))


def dot(a, b, dims):
    return lax.dot_general(a, b, dims, preferred_element_type=F32)


def rows_of(index, size):
    return pl.ds(pl.multiple_of(index * size, size), size)


def as_row(column):
    return jnp.broadcast_to(column, (256, 128)).T[0:8, :]


def as_column(row):
    return jnp.broadcast_to(row, (128, 256)).T


def kernel(
    up, inp, q, k, v, seg, gain, order, wq_hbm, wo_hbm,
    passed, qg, og, gg,
    upb, nms, nmz, wo, wq, probs, ao, aga, ag, qk,
    o_s, o_y1, o_y2, o_x, o_x1, o_x2,
    q_y, q_y1, q_y2,
    g_1, g_2, ssq, rowp, root, rtot, segc, gp, gz, gy, gx,
    lsem, ssem, rsem,
):
    sec = lax.axis_index("section")
    dp = lax.axis_index("dp")
    z = lax.axis_index("tensor")
    y = lax.div(dp, 4)
    x = lax.rem(dp, 4)

    z_to = [{"tensor": lax.rem(z + s, 4)} for s in range(4)]
    x_to = [{"dp": y * 4 + lax.rem(x + s, 4)} for s in range(4)]
    y_to = [{"dp": lax.rem(y + s, 4) * 4 + x} for s in range(4)]
    other = {"section": 1 - sec}

    counter = [0]
    sent = []

    def copy(src, dst, to, keep=True):
        index = counter[0]
        counter[0] += 1
        made = pltpu.make_async_remote_copy(
            src_ref=src,
            dst_ref=dst,
            send_sem=ssem.at[index],
            recv_sem=rsem.at[index],
            device_id=to,
            device_id_type=MESH,
        )
        if keep:
            sent.append(made)
        return made

    loads = [
        pltpu.make_async_copy(wo_hbm.at[:, pl.ds(1024 * b, 1024)], wo.at[b], lsem.at[b])
        for b in range(4)
    ]
    loads.append(pltpu.make_async_copy(wq_hbm, wq, lsem.at[4]))
    for one in loads:
        one.start()

    barrier = pltpu.get_barrier_semaphore()
    peers = z_to[1:] + x_to[1:] + y_to[1:] + [other]
    for peer in peers:
        pl.semaphore_signal(barrier, inc=1, device_id=peer, device_id_type=MESH)
    pl.semaphore_wait(barrier, len(peers))

    first, second = pl.ds(0, 256), pl.ds(256, 256)

    def gather(slots, to, a, b):
        own, right, far, left = slots
        return {
            "ra": copy(own.at[a], left.at[a], to[1]),
            "lb": copy(own.at[b], right.at[b], to[3]),
            "rb": copy(own.at[b], left.at[b], to[1]),
            "la": copy(own.at[a], right.at[a], to[3]),
            "fa": copy(left.at[a], far.at[a], to[1]),
            "fb": copy(right.at[b], far.at[b], to[3]),
        }

    def gather_start(made):
        for name in ("ra", "lb", "rb", "la"):
            made[name].start()

    def gather_relay(made):
        made["ra"].wait_recv()
        made["fa"].start()
        made["lb"].wait_recv()
        made["fb"].start()

    def gather_wait(made):
        for name in ("rb", "la", "fa", "fb"):
            made[name].wait_recv()

    def add_rows(dst, src, count, step=32):
        @pl.loop(0, count // step)
        def _(i):
            part = rows_of(i, step)
            dst[part, :] = (dst[part, :].astype(F32) + src[part, :].astype(F32)).astype(BF16)

    def scatter(far, right, left, half, land, full, to, keep=True):
        return {
            "a": copy(far.at[pl.ds(0, half)], land.at[0], to[1], keep),
            "b": copy(far.at[pl.ds(half, half)], land.at[1], to[3], keep),
            "r": copy(right, full.at[0], to[1], keep),
            "l": copy(left, full.at[1], to[3], keep),
            "add_a": (right.at[pl.ds(0, half)], land.at[0], half),
            "add_b": (left.at[pl.ds(half, half)], land.at[1], half),
        }

    def scatter_start(made):
        made["a"].start()
        made["b"].start()

    def scatter_mid(made):
        made["a"].wait_recv()
        add_rows(*made["add_a"])
        made["r"].start()
        made["b"].wait_recv()
        add_rows(*made["add_b"])
        made["l"].start()

    def scatter_wait(made):
        made["r"].wait_recv()
        made["l"].wait_recv()

    up_slots = [up, upb.at[0], upb.at[1], upb.at[2]]
    up_made = gather(up_slots, z_to, first, second)
    gather_start(up_made)

    for m in range(2):
        total = jnp.zeros((256, 1), F32)
        for c in range(4):
            wide = inp[pl.ds(256 * m, 256), pl.ds(256 * c, 256)].astype(F32)
            total += jnp.sum(wide * wide, axis=-1, keepdims=True)
        ssq[0, :, pl.ds(256 * m, 256)] = as_row(total)
    ssq_made = [copy(ssq.at[0], ssq.at[s], z_to[s]) for s in (1, 2, 3)]
    for one in ssq_made:
        one.start()

    for m in range(2):
        ids = seg[pl.ds(m, 1), :].astype(F32)
        segc[pl.ds(256 * m, 256), :] = jnp.broadcast_to(ids, (256, 256)).T

    @pl.loop(0, 8)
    def _(i):
        m = lax.div(i, 4)
        head = lax.rem(i, 4)
        rows = rows_of(m, 256)
        lanes = rows_of(lax.div(head, 2), 128)
        scores = dot(q[rows, rows_of(head, 128)], k[rows, lanes], NT) * SCALE
        low = lax.broadcasted_iota(jnp.int32, (256, 256), 0)
        high = lax.broadcasted_iota(jnp.int32, (256, 256), 1)
        ids = seg[pl.ds(m, 1), :].astype(F32)
        visible = (segc[rows, :] == ids) & (high <= low)
        scores = jnp.where(visible, scores, -1e30)
        top = jnp.max(scores, axis=-1, keepdims=True)
        shifted = jnp.where(visible, jnp.exp(scores - top), 0.0)
        weights = shifted / jnp.sum(shifted, axis=-1, keepdims=True)
        probs[i] = weights
        ao[rows, rows_of(head, 128)] = dot(weights.astype(BF16), v[rows, lanes], NN).astype(BF16)

    for one in loads[:4]:
        one.wait()

    def take_upstream(slot):
        block = lax.rem(z + slot, 4)
        ref = up_slots[slot]

        @pl.loop(0, 2)
        def _(m):
            rows = rows_of(m, 256)
            term = dot(ref[rows, :], wo[block], NT)
            if slot == 0:
                aga[rows, :] = term
            else:
                aga[rows, :] += term

    def out_terms(slot):
        block = lax.rem(z + slot, 4)
        ref = up_slots[slot]

        @pl.loop(0, 4)
        def _(j):
            lanes = rows_of(j, 256)
            o_s[block, :, lanes] = dot(ao[...], ref[:, lanes], TN).astype(BF16)

    take_upstream(0)
    gather_relay(up_made)
    out_terms(0)

    for one in ssq_made:
        one.wait_recv()
    for m in range(2):
        lanes = pl.ds(256 * m, 256)
        total = ssq[0, :, lanes] + ssq[1, :, lanes] + ssq[2, :, lanes] + ssq[3, :, lanes]
        root[lanes, :] = as_column(jnp.sqrt(total * (1.0 / 4096) + EPS)[0:1, :])

    for j in range(4):
        target = lax.rem(x + j, 4)
        lanes = rows_of(target, 256)
        part = gain[:, rows_of(z * 4 + target, 256)]
        kept = nmz.at[0, 0] if j == 0 else nms.at[j - 1]

        @pl.loop(0, 8)
        def _(i):
            rows = rows_of(i, 64)
            unit = inp[rows, lanes].astype(F32) / root[rows, 0:1]
            kept[rows, :] = (unit * part).astype(BF16)

    nx_made = [copy(nms.at[j - 1], nmz.at[0, 4 - j], x_to[j]) for j in (1, 2, 3)]
    for one in nx_made:
        one.start()

    up_made["rb"].wait_recv()
    take_upstream(3)
    out_terms(3)
    up_made["la"].wait_recv()
    take_upstream(1)
    out_terms(1)

    for one in nx_made:
        one.wait_recv()
    nm_made = gather([nmz.at[r] for r in range(4)], z_to, pl.ds(0, 2), pl.ds(2, 2))
    gather_start(nm_made)

    up_made["fa"].wait_recv()
    up_made["fb"].wait_recv()
    take_upstream(2)

    @pl.loop(0, 16)
    def _(i):
        rows = rows_of(i, 32)
        ag[rows, :] = aga[rows, :].astype(BF16)

    qk_made = [
        gather([qk.at[group, r] for r in range(4)], x_to, first, second) for group in range(2)
    ]
    for group in range(2):
        lanes = pl.ds(128 * group, 128)

        @pl.loop(0, 2)
        def _(m):
            rows = rows_of(m, 256)
            key_grad = jnp.zeros((256, 128), F32)
            value_grad = jnp.zeros((256, 128), F32)
            for h in range(2):
                head = pl.ds(128 * (group * 2 + h), 128)
                grad = ag[rows, head]
                weights = probs[m * 4 + group * 2 + h]
                probs_grad = dot(grad, v[rows, lanes], NT)
                row_dot = jnp.sum(weights * probs_grad, axis=-1, keepdims=True)
                score_grad = (weights * (probs_grad - row_dot) * SCALE).astype(BF16)
                qk[group, 0, rows, pl.ds(128 * h, 128)] = dot(score_grad, k[rows, lanes], NN).astype(BF16)
                key_grad += dot(score_grad, q[rows, head], TN)
                value_grad += dot(weights.astype(BF16), grad, TN)
            qk[group, 0, rows, pl.ds(256, 128)] = key_grad.astype(BF16)
            qk[group, 0, rows, pl.ds(384, 128)] = value_grad.astype(BF16)

        gather_start(qk_made[group])

    gather_relay(nm_made)
    out_terms(2)
    o_made = scatter(
        o_s.at[lax.rem(y + 2, 4)], o_s.at[lax.rem(y + 1, 4)], o_s.at[lax.rem(y + 3, 4)],
        256, o_y1, o_y2, y_to,
    )
    scatter_start(o_made)
    gather_relay(qk_made[0])
    loads[4].wait()

    q_made = [
        scatter(
            q_y.at[group, lax.rem(y + 2, 4)], q_y.at[group, lax.rem(y + 1, 4)],
            q_y.at[group, lax.rem(y + 3, 4)], 128, q_y1.at[group], q_y2.at[group], y_to,
        )
        for group in range(2)
    ]

    def qkv_terms(group):
        def one(j):
            block = lax.rem(y + j + 2, 4)
            slot = lax.rem(block - z + 4, 4)
            term = dot(nmz[slot].reshape(2048, 256), qk[group].reshape(2048, 512), TN)
            weight = wq[block, rows_of(x, 256), pl.ds(512 * group, 512)].astype(F32)
            row = as_row(jnp.sum(term * weight, axis=-1, keepdims=True))
            if group == 0:
                gp[slot] = row
            else:
                gp[slot] += row
            q_y[group, block] = term.astype(BF16)

        one(0)
        scatter_start(q_made[group])
        pl.loop(1, 4)(one)

    z_made = scatter(wo.at[2], wo.at[1], wo.at[3], 256, g_1, g_2, z_to, keep=False)

    @pl.when(sec == 1)
    def _():
        @pl.loop(0, 16)
        def _(i):
            j = lax.div(i, 4)
            part = rows_of(lax.rem(i, 4), 256)
            at = lax.rem(z + j, 4)
            term = dot(qk[0, 0], wq[at, part, pl.ds(0, 512)], NT)
            term += dot(qk[1, 0], wq[at, part, pl.ds(512, 512)], NT)
            wo[j, :, part] = term.astype(BF16)

        scatter_start(z_made)

    gather_relay(qk_made[1])
    scatter_mid(o_made)
    gather_wait(nm_made)
    gather_wait(qk_made[0])
    qkv_terms(0)

    @pl.when(sec == 1)
    def _():
        scatter_mid(z_made)

    gather_wait(qk_made[1])
    qkv_terms(1)

    gz_made = [copy(gp.at[r], gz.at[r - 1], z_to[r]) for r in (1, 2, 3)]
    for one in gz_made:
        one.start()

    scatter_wait(o_made)
    o_own = o_s.at[y]

    @pl.loop(0, 4)
    def _(j):
        lanes = rows_of(lax.rem(x + j, 4), 256)

        @pl.loop(0, 8)
        def _(i):
            rows = rows_of(i, 64)
            total = (
                o_own[rows, lanes].astype(F32)
                + o_y2[0, rows, lanes].astype(F32)
                + o_y2[1, rows, lanes].astype(F32)
            )
            o_x[j, rows, :] = total.astype(BF16)

    ox_made = scatter(o_x.at[2], o_x.at[1], o_x.at[3], 256, o_x1, o_x2, x_to)
    scatter_start(ox_made)
    scatter_mid(q_made[0])

    for one in gz_made:
        one.wait_recv()
    gy[0] = gp[0] + gz[0] + gz[1] + gz[2]
    gy_made = [copy(gy.at[0], gy.at[s], y_to[s]) for s in (1, 2, 3)]
    for one in gy_made:
        one.start()

    layer = upb.at[1]
    row_made = [copy(rowp.at[0], rowp.at[s], z_to[s], keep=False) for s in (1, 2, 3)]

    def scaled_unit(rows):
        grad = (
            wo[0, rows, :].astype(F32) + g_2[0, rows, :].astype(F32) + g_2[1, rows, :].astype(F32)
        )
        return grad * gain[:, rows_of(z, 1024)], inp[rows, :].astype(F32) / root[rows, 0:1]

    @pl.when(sec == 1)
    def _():
        scatter_wait(z_made)

        @pl.loop(0, 16)
        def _(i):
            rows = rows_of(i, 32)
            scaled, unit = scaled_unit(rows)
            part = jnp.sum(scaled * unit, axis=-1, keepdims=True)
            rtot[rows, :] = jnp.broadcast_to(part, (32, 128))

        for m in range(2):
            lanes = pl.ds(256 * m, 256)
            rowp[0, :, lanes] = rtot[lanes, :].T[0:8, :]
        for one in row_made:
            one.start()

    scatter_mid(ox_made)
    scatter_mid(q_made[1])

    for one in gy_made:
        one.wait_recv()
    gx[x] = (gy[0] + gy[1] + gy[2] + gy[3]) / (gain[:, rows_of(z * 4 + x, 256)] * 16.0)
    gx_made = [copy(gx.at[x], gx.at[x], x_to[s]) for s in (1, 2, 3)]
    for one in gx_made:
        one.start()

    passed_made = copy(layer, passed, other, keep=False)

    @pl.when(sec == 1)
    def _():
        for one in row_made:
            one.wait_recv()
        for m in range(2):
            lanes = pl.ds(256 * m, 256)
            total = rowp[0, :, lanes] + rowp[1, :, lanes] + rowp[2, :, lanes] + rowp[3, :, lanes]
            rtot[lanes, :] = as_column((total * (1.0 / 4096))[0:1, :])
        straight = order[0:1, 0:1] == 0

        @pl.loop(0, 16)
        def _(i):
            both = []
            for m in range(2):
                rows = pl.ds(pl.multiple_of(m * 256 + i * 16, 16), 16)
                scaled, unit = scaled_unit(rows)
                through = up[rows, :].astype(F32) + (scaled - unit * rtot[rows, 0:1]) / root[rows, 0:1]
                both.append(through)
            low, high = both
            keep_order = jnp.broadcast_to(straight, (16, 1024))
            rows = pl.ds(pl.multiple_of(i * 16, 16), 16)
            layer[rows, :] = jnp.where(keep_order, low, high).astype(BF16)
            rows = pl.ds(pl.multiple_of(256 + i * 16, 16), 16)
            layer[rows, :] = jnp.where(keep_order, high, low).astype(BF16)

        passed_made.start()

        @pl.loop(0, 16)
        def _(i):
            passed[rows_of(i, 32), :] = jnp.zeros((32, 1024), BF16)

    scatter_wait(ox_made)

    @pl.loop(0, 8)
    def _(i):
        rows = rows_of(i, 64)
        total = o_x[0, rows, :].astype(F32) + o_x2[0, rows, :].astype(F32) + o_x2[1, rows, :].astype(F32)
        og[rows, :] = total * (1.0 / 16)

    for one in gx_made:
        one.wait_recv()
    for s in range(4):
        gg[:, pl.ds(256 * s, 256)] = gx[s]

    for group in range(2):
        scatter_wait(q_made[group])

        @pl.loop(0, 4)
        def _(i):
            rows = rows_of(i, 64)
            total = (
                q_y[group, y, rows, :].astype(F32)
                + q_y2[group, 0, rows, :].astype(F32)
                + q_y2[group, 1, rows, :].astype(F32)
            )
            qg[rows, pl.ds(512 * group, 512)] = total * (1.0 / 16)

    @pl.when(sec == 0)
    def _():
        passed_made.wait_recv()

    @pl.when(sec == 1)
    def _():
        for one in [z_made[name] for name in "abrl"] + row_made + [passed_made]:
            one.wait_send()

    for one in sent:
        one.wait_send()


def shards(
    layer_input,
    norm_gain,
    upstream_grad,
    saved_queries,
    saved_keys,
    saved_values,
    segment_ids,
    batch_order,
    qkv_weight,
    out_weight,
):
    def by_micro(array):
        return array[0].transpose(1, 0, 2).reshape(512, array.shape[3])

    vmem = pl.BlockSpec(memory_space=pltpu.VMEM)
    hbm = pl.BlockSpec(memory_space=pl.ANY)
    passed, qkv_grad, out_grad, gain_grad = pl.pallas_call(
        kernel,
        out_shape=(
            jax.ShapeDtypeStruct((512, 1024), BF16),
            jax.ShapeDtypeStruct((256, 1024), F32),
            jax.ShapeDtypeStruct((512, 256), F32),
            jax.ShapeDtypeStruct((8, 1024), F32),
        ),
        in_specs=[vmem] * 8 + [hbm] * 2,
        out_specs=(vmem,) * 4,
        scratch_shapes=[
            pltpu.VMEM((3, 512, 1024), BF16),
            pltpu.VMEM((3, 512, 256), BF16),
            pltpu.VMEM((4, 4, 512, 256), BF16),
            pltpu.VMEM((4, 512, 1024), BF16),
            pltpu.VMEM((4, 1024, 1024), BF16),
            pltpu.VMEM((8, 256, 256), F32),
            pltpu.VMEM((512, 512), BF16),
            pltpu.VMEM((512, 512), F32),
            pltpu.VMEM((512, 512), BF16),
            pltpu.VMEM((2, 4, 512, 512), BF16),
            pltpu.VMEM((4, 512, 1024), BF16),
            pltpu.VMEM((2, 256, 1024), BF16),
            pltpu.VMEM((2, 512, 1024), BF16),
            pltpu.VMEM((4, 512, 256), BF16),
            pltpu.VMEM((2, 256, 256), BF16),
            pltpu.VMEM((2, 512, 256), BF16),
            pltpu.VMEM((2, 4, 256, 512), BF16),
            pltpu.VMEM((2, 2, 128, 512), BF16),
            pltpu.VMEM((2, 2, 256, 512), BF16),
            pltpu.VMEM((2, 256, 1024), BF16),
            pltpu.VMEM((2, 512, 1024), BF16),
            pltpu.VMEM((4, 8, 512), F32),
            pltpu.VMEM((4, 8, 512), F32),
            pltpu.VMEM((512, 128), F32),
            pltpu.VMEM((512, 128), F32),
            pltpu.VMEM((512, 256), F32),
            pltpu.VMEM((4, 8, 256), F32),
            pltpu.VMEM((3, 8, 256), F32),
            pltpu.VMEM((4, 8, 256), F32),
            pltpu.VMEM((4, 8, 256), F32),
            pltpu.SemaphoreType.DMA((5,)),
            pltpu.SemaphoreType.DMA((80,)),
            pltpu.SemaphoreType.DMA((80,)),
        ],
        compiler_params=pltpu.CompilerParams(
            collective_id=0, has_side_effects=True, vmem_limit_bytes=67043328
        ),
    )(
        by_micro(upstream_grad),
        by_micro(layer_input),
        by_micro(saved_queries),
        by_micro(saved_keys),
        by_micro(saved_values),
        segment_ids[0],
        norm_gain,
        batch_order[0],
        qkv_weight[0].reshape(4, 1024, 1024),
        out_weight[0],
    )
    passed = passed.reshape(2, 256, 1024).transpose(1, 0, 2)
    return (passed[None], qkv_grad[None], out_grad[None], gain_grad[0:1])


def solution(mesh):
    placed = (
        P("section", "dp", None, "tensor"),
        P("section", None),
        P("section", "dp", None, "tensor"),
        P("section", "dp", None, "tensor"),
        P("section", "dp", None, "tensor"),
        P("section", "dp", None, "tensor"),
        P("section", None, "dp"),
        P("section", "dp", None),
        P("section", None, "tensor"),
        P("section", "tensor", None),
    )
    return jax.shard_map(
        shards,
        mesh=mesh,
        in_specs=placed,
        out_specs=(
            P("section", "dp", None, "tensor"),
            P("section", "dp", "tensor"),
            P("section", "tensor", "dp"),
            P("section", "tensor"),
        ),
        check_vma=False,
    )
```

```python
import math

import jax
import jax.numpy as jnp
from jax import lax
from jax.experimental import pallas as pl
from jax.experimental.pallas import tpu as pltpu
from jax.sharding import PartitionSpec as P

HD = 128
EPS = 1e-05
MESH = pl.DeviceIdType.MESH
F32 = jnp.float32
BF16 = jnp.bfloat16
SIX = ("fa", "fb", "rb", "la", "ra", "lb")
SCALE = 1.0 / math.sqrt(HD)

NT = (((1,), (1,)), ((), ()))
NN = (((1,), (0,)), ((), ()))
TN = (((0,), (0,)), ((), ()))


def dot(a, b, dims):
    return lax.dot_general(a, b, dims, preferred_element_type=F32)


def rows_of(index, size):
    return pl.ds(pl.multiple_of(index * size, size), size)


def as_row(column):
    return jnp.broadcast_to(column, (256, 128)).T[0:8, :]


def as_column(row):
    return jnp.broadcast_to(row, (128, 256)).T


def kernel(
    up_hbm, inp_hbm, q_hbm, k_hbm, v_hbm, seg, gain, order, wq_hbm, wo_hbm,
    passed, qg, og, gg,
    upb, nms, nmz, wo, wq, probs, ao, aga, ag, qk,
    o_s, o_y1, o_y2, o_x, o_x1, o_x2,
    q_y, q_y1, q_y2,
    g_1, g_2, ssq, rowp, root, rtot, segc, gp, gz, gy, gx,
    up_raw, inp_raw, q_raw, k_raw, v_raw, up, inp, q, k, v, un,
    lsem, ssem, rsem,
):
    sec = lax.axis_index("section")
    dp = lax.axis_index("dp")
    z = lax.axis_index("tensor")
    y = lax.div(dp, 4)
    x = lax.rem(dp, 4)

    z_to = [{"tensor": lax.rem(z + s, 4)} for s in range(4)]
    x_to = [{"dp": y * 4 + lax.rem(x + s, 4)} for s in range(4)]
    y_to = [{"dp": lax.rem(y + s, 4) * 4 + x} for s in range(4)]
    other = {"section": 1 - sec}

    counter = [0]
    sent = []

    def copy(src, dst, to, keep=True):
        index = counter[0]
        counter[0] += 1
        made = pltpu.make_async_remote_copy(
            src_ref=src,
            dst_ref=dst,
            send_sem=ssem.at[index],
            recv_sem=rsem.at[index],
            device_id=to,
            device_id_type=MESH,
        )
        if keep:
            sent.append(made)
        return made

    stored = ((up_hbm, up_raw, up), (inp_hbm, inp_raw, inp), (q_hbm, q_raw, q), (k_hbm, k_raw, k), (v_hbm, v_raw, v))
    fetches = [
        pltpu.make_async_copy(source, raw, lsem.at[5 + i]) for i, (source, raw, _) in enumerate(stored)
    ]
    loads = [
        pltpu.make_async_copy(wo_hbm.at[:, pl.ds(1024 * b, 1024)], wo.at[b], lsem.at[b])
        for b in range(4)
    ]
    loads.append(pltpu.make_async_copy(wq_hbm, wq, lsem.at[4]))
    for one in fetches + loads:
        one.start()

    def by_micro(which):
        fetches[which].wait()
        _, raw, kept = stored[which]

        @pl.loop(0, 16)
        def _(i):
            for m in range(2):
                kept[pl.ds(pl.multiple_of(256 * m + i * 16, 16), 16), :] = raw[rows_of(i, 16), m, :]

    barrier = pltpu.get_barrier_semaphore()
    peers = z_to[1:] + x_to[1:] + y_to[1:] + [other]
    for peer in peers:
        pl.semaphore_signal(barrier, inc=1, device_id=peer, device_id_type=MESH)
    pl.semaphore_wait(barrier, len(peers))

    first, second = pl.ds(0, 256), pl.ds(256, 256)

    def gather(slots, to, a, b):
        own, right, far, left = slots
        return {
            "ra": copy(own.at[a], left.at[a], to[1]),
            "lb": copy(own.at[b], right.at[b], to[3]),
            "rb": copy(own.at[b], left.at[b], to[1]),
            "la": copy(own.at[a], right.at[a], to[3]),
            "fa": copy(left.at[a], far.at[a], to[1]),
            "fb": copy(right.at[b], far.at[b], to[3]),
        }

    def gather_start(made):
        for name in ("ra", "lb", "rb", "la"):
            made[name].start()

    def gather_relay(made):
        made["ra"].wait_recv()
        made["fa"].start()
        made["lb"].wait_recv()
        made["fb"].start()

    def gather_wait(made):
        for name in ("rb", "la", "fa", "fb"):
            made[name].wait_recv()

    def add_rows(dst, src, count, step=32):
        @pl.loop(0, count // step)
        def _(i):
            part = rows_of(i, step)
            dst[part, :] = (dst[part, :].astype(F32) + src[part, :].astype(F32)).astype(BF16)

    def scatter(far, right, left, half, land, full, to, keep=True):
        a, b = pl.ds(0, half), pl.ds(half, half)
        return {
            "fa": copy(far.at[a], land.at[0], to[1], keep),
            "fb": copy(far.at[b], land.at[1], to[3], keep),
            "rb": copy(right.at[b], full.at[0, b], to[1], keep),
            "la": copy(left.at[a], full.at[1, a], to[3], keep),
            "ra": copy(right.at[a], full.at[0, a], to[1], keep),
            "lb": copy(left.at[b], full.at[1, b], to[3], keep),
            "add_a": (right.at[a], land.at[0], half),
            "add_b": (left.at[b], land.at[1], half),
        }

    def scatter_start(made):
        for name in ("fa", "fb", "rb", "la"):
            made[name].start()

    def scatter_mid_a(made):
        made["fa"].wait_recv()
        add_rows(*made["add_a"])
        made["ra"].start()

    def scatter_mid_b(made):
        made["fb"].wait_recv()
        add_rows(*made["add_b"])
        made["lb"].start()

    def scatter_mid(made):
        scatter_mid_a(made)
        scatter_mid_b(made)

    def scatter_wait(made):
        for name in ("rb", "la", "ra", "lb"):
            made[name].wait_recv()

    up_slots = [up, upb.at[0], upb.at[1], upb.at[2]]
    up_made = gather(up_slots, z_to, first, second)
    by_micro(0)
    up_made["ra"].start()
    up_made["lb"].start()
    by_micro(1)

    for m in range(2):
        total = jnp.zeros((256, 1), F32)
        for c in range(4):
            wide = inp[pl.ds(256 * m, 256), pl.ds(256 * c, 256)].astype(F32)
            total += jnp.sum(wide * wide, axis=-1, keepdims=True)
        ssq[0, :, pl.ds(256 * m, 256)] = as_row(total)
    ssq_made = [copy(ssq.at[0], ssq.at[s], z_to[s]) for s in (1, 2, 3)]
    for one in ssq_made:
        one.start()
    up_made["rb"].start()
    up_made["la"].start()
    for which in (2, 3, 4):
        by_micro(which)

    for m in range(2):
        ids = seg[pl.ds(m, 1), :].astype(F32)
        segc[pl.ds(256 * m, 256), :] = jnp.broadcast_to(ids, (256, 256)).T

    @pl.loop(0, 8)
    def _(i):
        m = lax.div(i, 4)
        head = lax.rem(i, 4)
        rows = rows_of(m, 256)
        lanes = rows_of(lax.div(head, 2), 128)
        scores = dot(q[rows, rows_of(head, 128)], k[rows, lanes], NT) * SCALE
        low = lax.broadcasted_iota(jnp.int32, (256, 256), 0)
        high = lax.broadcasted_iota(jnp.int32, (256, 256), 1)
        ids = seg[pl.ds(m, 1), :].astype(F32)
        visible = (segc[rows, :] == ids) & (high <= low)
        scores = jnp.where(visible, scores, -1e30)
        top = jnp.max(scores, axis=-1, keepdims=True)
        shifted = jnp.where(visible, jnp.exp(scores - top), 0.0)
        weights = shifted / jnp.sum(shifted, axis=-1, keepdims=True)
        probs[i] = weights
        ao[rows_of(head, 128), rows] = dot(weights.astype(BF16), v[rows, lanes], NN).T.astype(BF16)

    for one in loads[:4]:
        one.wait()

    def take_upstream(slot):
        block = lax.rem(z + slot, 4)
        ref = up_slots[slot]

        @pl.loop(0, 2)
        def _(m):
            rows = rows_of(m, 256)
            term = dot(ref[rows, :], wo[block], NT)
            if slot == 0:
                aga[rows, :] = term
            elif slot == 2:
                ag[rows, :] = (aga[rows, :] + term).astype(BF16)
            else:
                aga[rows, :] += term

    o_made = scatter(
        o_s.at[lax.rem(y + 2, 4)], o_s.at[lax.rem(y + 1, 4)], o_s.at[lax.rem(y + 3, 4)],
        256, o_y1, o_y2, y_to,
    )

    def out_terms(slot):
        block = lax.rem(z + slot, 4)
        ref = up_slots[slot]

        @pl.loop(0, 4)
        def _(j):
            lanes = rows_of(j, 256)
            o_s[block, :, lanes] = dot(ao[...], ref[:, lanes], NN).astype(BF16)

        role = lax.rem(block - y + 4, 4)

        @pl.when(role == 2)
        def _():
            o_made["fa"].start()
            o_made["fb"].start()

        @pl.when(role == 1)
        def _():
            o_made["rb"].start()

        @pl.when(role == 3)
        def _():
            o_made["la"].start()

    def out_mid(slot):
        role = lax.rem(lax.rem(z + slot, 4) - y + 4, 4)

        @pl.when(role == 1)
        def _():
            scatter_mid_a(o_made)

        @pl.when(role == 3)
        def _():
            scatter_mid_b(o_made)

    take_upstream(0)
    out_terms(0)
    gather_relay(up_made)

    for one in ssq_made:
        one.wait_recv()
    for m in range(2):
        lanes = pl.ds(256 * m, 256)
        total = ssq[0, :, lanes] + ssq[1, :, lanes] + ssq[2, :, lanes] + ssq[3, :, lanes]
        root[lanes, :] = as_column((1.0 / jnp.sqrt(total * (1.0 / 4096) + EPS))[0:1, :])

    for j in range(4):
        target = lax.rem(x + j, 4)
        lanes = rows_of(target, 256)
        part = gain[:, rows_of(z * 4 + target, 256)]
        kept = nmz.at[0, 0] if j == 0 else nms.at[j - 1]

        @pl.loop(0, 4)
        def _(i):
            rows = rows_of(i, 128)
            unit = inp[rows, lanes].astype(F32) * root[rows, 0:1]
            un[rows, lanes] = unit
            kept[:, rows] = (unit * part).T.astype(BF16)

    nx_made = [copy(nms.at[j - 1], nmz.at[0, 4 - j], x_to[j]) for j in (1, 2, 3)]
    for one in nx_made:
        one.start()

    up_made["rb"].wait_recv()
    take_upstream(3)
    out_terms(3)
    up_made["la"].wait_recv()
    take_upstream(1)
    out_terms(1)

    for one in nx_made:
        one.wait_recv()
    nm_made = gather([nmz.at[r] for r in range(4)], z_to, pl.ds(0, 2), pl.ds(2, 2))
    gather_start(nm_made)

    up_made["fa"].wait_recv()
    up_made["fb"].wait_recv()
    take_upstream(2)

    out_mid(0)

    qk_made = [
        gather([qk.at[group, r] for r in range(4)], x_to, first, second) for group in range(2)
    ]
    for group in range(2):
        lanes = pl.ds(128 * group, 128)

        @pl.loop(0, 2)
        def _(m):
            rows = rows_of(m, 256)
            key_grad = jnp.zeros((256, 128), F32)
            value_grad = jnp.zeros((256, 128), F32)
            for h in range(2):
                head = pl.ds(128 * (group * 2 + h), 128)
                grad = ag[rows, head]
                weights = probs[m * 4 + group * 2 + h]
                probs_grad = dot(grad, v[rows, lanes], NT)
                row_dot = jnp.sum(weights * probs_grad, axis=-1, keepdims=True)
                score_grad = (weights * (probs_grad - row_dot) * SCALE).astype(BF16)
                qk[group, 0, rows, pl.ds(128 * h, 128)] = dot(score_grad, k[rows, lanes], NN).astype(BF16)
                key_grad += dot(score_grad, q[rows, head], TN)
                value_grad += dot(weights.astype(BF16), grad, TN)
            qk[group, 0, rows, pl.ds(256, 128)] = key_grad.astype(BF16)
            qk[group, 0, rows, pl.ds(384, 128)] = value_grad.astype(BF16)

        gather_start(qk_made[group])

    out_terms(2)
    out_mid(3)
    out_mid(1)
    gather_relay(nm_made)
    gather_relay(qk_made[0])
    loads[4].wait()

    q_made = [
        scatter(
            q_y.at[group, lax.rem(y + 2, 4)], q_y.at[group, lax.rem(y + 1, 4)],
            q_y.at[group, lax.rem(y + 3, 4)], 128, q_y1.at[group], q_y2.at[group], y_to,
        )
        for group in range(2)
    ]

    def qkv_terms(group):
        for j in (2, 1, 3, 0):
            block = lax.rem(y + j, 4)
            slot = lax.rem(block - z + 4, 4)
            normed = jnp.concatenate([nmz[slot, r] for r in range(4)], axis=1)
            term = dot(normed, qk[group].reshape(2048, 512), NN)
            q_y[group, block] = term.astype(BF16)
            if j == 2:
                q_made[group]["fa"].start()
                q_made[group]["fb"].start()
            elif j == 1:
                q_made[group]["rb"].start()
            elif j == 3:
                q_made[group]["la"].start()
            weight = wq[block, rows_of(x, 256), pl.ds(512 * group, 512)].astype(F32)
            row = as_row(jnp.sum(term * weight, axis=-1, keepdims=True))
            if group == 0:
                gp[slot] = row
            else:
                gp[slot] += row

    z_made = scatter(wo.at[2], wo.at[1], wo.at[3], 256, g_1, g_2, z_to, keep=False)

    @pl.when(sec == 1)
    def _():
        @pl.loop(0, 16)
        def _(i):
            j = lax.div(i, 4)
            part = rows_of(lax.rem(i, 4), 256)
            at = lax.rem(z + j, 4)
            term = dot(qk[0, 0], wq[at, part, pl.ds(0, 512)], NT)
            term += dot(qk[1, 0], wq[at, part, pl.ds(512, 512)], NT)
            wo[j, :, part] = term.astype(BF16)

        scatter_start(z_made)

    gather_relay(qk_made[1])
    out_mid(2)
    gather_wait(nm_made)
    gather_wait(qk_made[0])
    qkv_terms(0)

    @pl.when(sec == 1)
    def _():
        scatter_mid(z_made)

    gather_wait(qk_made[1])
    qkv_terms(1)

    gz_made = [copy(gp.at[r], gz.at[r - 1], z_to[r]) for r in (1, 2, 3)]
    for one in gz_made:
        one.start()

    scatter_wait(o_made)
    o_own = o_s.at[y]

    @pl.loop(0, 4)
    def _(j):
        lanes = rows_of(lax.rem(x + j, 4), 256)

        @pl.loop(0, 8)
        def _(i):
            rows = rows_of(i, 64)
            total = (
                o_own[rows, lanes].astype(F32)
                + o_y2[0, rows, lanes].astype(F32)
                + o_y2[1, rows, lanes].astype(F32)
            )
            o_x[j, rows, :] = total.astype(BF16)

    ox_made = scatter(o_x.at[2], o_x.at[1], o_x.at[3], 256, o_x1, o_x2, x_to)
    scatter_start(ox_made)
    scatter_mid(q_made[0])

    for one in gz_made:
        one.wait_recv()
    gy[0] = gp[0] + gz[0] + gz[1] + gz[2]
    gy_made = [copy(gy.at[0], gy.at[s], y_to[s]) for s in (1, 2, 3)]
    for one in gy_made:
        one.start()

    layer = upb.at[1]
    row_made = [copy(rowp.at[0], rowp.at[s], z_to[s], keep=False) for s in (1, 2, 3)]

    def scaled_unit(rows):
        grad = (
            wo[0, rows, :].astype(F32) + g_2[0, rows, :].astype(F32) + g_2[1, rows, :].astype(F32)
        )
        return grad * gain[:, rows_of(z, 1024)], un[rows, :]

    @pl.when(sec == 1)
    def _():
        scatter_wait(z_made)

        @pl.loop(0, 16)
        def _(i):
            rows = rows_of(i, 32)
            scaled, unit = scaled_unit(rows)
            part = jnp.sum(scaled * unit, axis=-1, keepdims=True)
            rtot[rows, :] = jnp.broadcast_to(part, (32, 128))

        for m in range(2):
            lanes = pl.ds(256 * m, 256)
            rowp[0, :, lanes] = rtot[lanes, :].T[0:8, :]
        for one in row_made:
            one.start()

    scatter_mid(ox_made)
    scatter_mid(q_made[1])

    for one in gy_made:
        one.wait_recv()
    gx[x] = (gy[0] + gy[1] + gy[2] + gy[3]) / (gain[:, rows_of(z * 4 + x, 256)] * 16.0)
    gx_made = [copy(gx.at[x], gx.at[x], x_to[s]) for s in (1, 2, 3)]
    for one in gx_made:
        one.start()

    pieces = [pl.ds(128 * i, 128) for i in range(4)]
    passed_made = [copy(layer.at[piece], passed.at[piece], other, keep=False) for piece in pieces]

    @pl.when(sec == 1)
    def _():
        for one in row_made:
            one.wait_recv()
        for m in range(2):
            lanes = pl.ds(256 * m, 256)
            total = rowp[0, :, lanes] + rowp[1, :, lanes] + rowp[2, :, lanes] + rowp[3, :, lanes]
            rtot[lanes, :] = as_column((total * (1.0 / 4096))[0:1, :])
        straight = order[0:1, 0:1] == 0

        for half in range(2):

            @pl.loop(8 * half, 8 * half + 8)
            def _(i):
                both = []
                for m in range(2):
                    rows = pl.ds(pl.multiple_of(m * 256 + i * 16, 16), 16)
                    scaled, unit = scaled_unit(rows)
                    through = up[rows, :].astype(F32) + (scaled - unit * rtot[rows, 0:1]) * root[rows, 0:1]
                    both.append(through)
                low, high = both
                keep_order = jnp.broadcast_to(straight, (16, 1024))
                rows = pl.ds(pl.multiple_of(i * 16, 16), 16)
                layer[rows, :] = jnp.where(keep_order, low, high).astype(BF16)
                rows = pl.ds(pl.multiple_of(256 + i * 16, 16), 16)
                layer[rows, :] = jnp.where(keep_order, high, low).astype(BF16)

            passed_made[half].start()
            passed_made[half + 2].start()

        @pl.loop(0, 16)
        def _(i):
            passed[rows_of(i, 32), :] = jnp.zeros((32, 1024), BF16)

    scatter_wait(ox_made)

    @pl.loop(0, 8)
    def _(i):
        rows = rows_of(i, 64)
        total = o_x[0, rows, :].astype(F32) + o_x2[0, rows, :].astype(F32) + o_x2[1, rows, :].astype(F32)
        og[rows, :] = total * (1.0 / 16)

    for one in gx_made:
        one.wait_recv()
    for s in range(4):
        gg[:, pl.ds(256 * s, 256)] = gx[s]

    for group in range(2):
        scatter_wait(q_made[group])

        @pl.loop(0, 4)
        def _(i):
            rows = rows_of(i, 64)
            total = (
                q_y[group, y, rows, :].astype(F32)
                + q_y2[group, 0, rows, :].astype(F32)
                + q_y2[group, 1, rows, :].astype(F32)
            )
            qg[rows, pl.ds(512 * group, 512)] = total * (1.0 / 16)

    @pl.when(sec == 0)
    def _():
        for one in passed_made:
            one.wait_recv()

    @pl.when(sec == 1)
    def _():
        for one in [z_made[name] for name in SIX] + row_made + passed_made:
            one.wait_send()

    for one in sent:
        one.wait_send()


def finish(passed, qkv_sum, out_sum, gain_sum, passed_out, qkv_out, out_out, gain_out):
    @pl.loop(0, 4)
    def _(i):
        rows = rows_of(i, 16)
        low, high = passed[0, rows, :].astype(F32), passed[1, rows, :].astype(F32)
        passed_out[rows] = jnp.stack([low, high], axis=1).astype(BF16)

    qkv_out[...] = qkv_sum[...]
    out_out[...] = out_sum[...]
    gain_out[...] = gain_sum[0:1, :]


def shards(
    layer_input,
    norm_gain,
    upstream_grad,
    saved_queries,
    saved_keys,
    saved_values,
    segment_ids,
    batch_order,
    qkv_weight,
    out_weight,
):
    vmem = pl.BlockSpec(memory_space=pltpu.VMEM)
    hbm = pl.BlockSpec(memory_space=pl.ANY)
    passed, qkv_grad, out_grad, gain_grad = pl.pallas_call(
        kernel,
        out_shape=(
            jax.ShapeDtypeStruct((512, 1024), BF16),
            jax.ShapeDtypeStruct((256, 1024), F32),
            jax.ShapeDtypeStruct((512, 256), F32),
            jax.ShapeDtypeStruct((8, 1024), F32),
        ),
        in_specs=[hbm] * 5 + [vmem] * 3 + [hbm] * 2,
        out_specs=(vmem,) * 4,
        scratch_shapes=[
            pltpu.VMEM((3, 512, 1024), BF16),
            pltpu.VMEM((3, 256, 512), BF16),
            pltpu.VMEM((4, 4, 256, 512), BF16),
            pltpu.VMEM((4, 512, 1024), BF16),
            pltpu.VMEM((4, 1024, 1024), BF16),
            pltpu.VMEM((8, 256, 256), F32),
            pltpu.VMEM((512, 512), BF16),
            pltpu.VMEM((512, 512), F32),
            pltpu.VMEM((512, 512), BF16),
            pltpu.VMEM((2, 4, 512, 512), BF16),
            pltpu.VMEM((4, 512, 1024), BF16),
            pltpu.VMEM((2, 256, 1024), BF16),
            pltpu.VMEM((2, 512, 1024), BF16),
            pltpu.VMEM((4, 512, 256), BF16),
            pltpu.VMEM((2, 256, 256), BF16),
            pltpu.VMEM((2, 512, 256), BF16),
            pltpu.VMEM((2, 4, 256, 512), BF16),
            pltpu.VMEM((2, 2, 128, 512), BF16),
            pltpu.VMEM((2, 2, 256, 512), BF16),
            pltpu.VMEM((2, 256, 1024), BF16),
            pltpu.VMEM((2, 512, 1024), BF16),
            pltpu.VMEM((4, 8, 512), F32),
            pltpu.VMEM((4, 8, 512), F32),
            pltpu.VMEM((512, 128), F32),
            pltpu.VMEM((512, 128), F32),
            pltpu.VMEM((512, 256), F32),
            pltpu.VMEM((4, 8, 256), F32),
            pltpu.VMEM((3, 8, 256), F32),
            pltpu.VMEM((4, 8, 256), F32),
            pltpu.VMEM((4, 8, 256), F32),
            pltpu.VMEM((256, 2, 1024), BF16),
            pltpu.VMEM((256, 2, 1024), BF16),
            pltpu.VMEM((256, 2, 512), BF16),
            pltpu.VMEM((256, 2, 256), BF16),
            pltpu.VMEM((256, 2, 256), BF16),
            pltpu.VMEM((512, 1024), BF16),
            pltpu.VMEM((512, 1024), BF16),
            pltpu.VMEM((512, 512), BF16),
            pltpu.VMEM((512, 256), BF16),
            pltpu.VMEM((512, 256), BF16),
            pltpu.VMEM((512, 1024), F32),
            pltpu.SemaphoreType.DMA((10,)),
            pltpu.SemaphoreType.DMA((90,)),
            pltpu.SemaphoreType.DMA((90,)),
        ],
        compiler_params=pltpu.CompilerParams(
            collective_id=0, has_side_effects=True, vmem_limit_bytes=67043328
        ),
    )(
        upstream_grad[0],
        layer_input[0],
        saved_queries[0],
        saved_keys[0],
        saved_values[0],
        segment_ids[0],
        norm_gain,
        batch_order[0],
        qkv_weight[0].reshape(4, 1024, 1024),
        out_weight[0],
    )
    passed, qkv_grad, out_grad, gain_grad = pl.pallas_call(
        finish,
        grid=(4,),
        out_shape=(
            jax.ShapeDtypeStruct((256, 2, 1024), BF16),
            jax.ShapeDtypeStruct((256, 1024), F32),
            jax.ShapeDtypeStruct((512, 256), F32),
            jax.ShapeDtypeStruct((1, 1024), F32),
        ),
        in_specs=[
            pl.BlockSpec((2, 64, 1024), lambda i: (0, i, 0)),
            pl.BlockSpec((64, 1024), lambda i: (i, 0)),
            pl.BlockSpec((128, 256), lambda i: (i, 0)),
            pl.BlockSpec((8, 1024), lambda i: (0, 0)),
        ],
        out_specs=(
            pl.BlockSpec((64, 2, 1024), lambda i: (i, 0, 0)),
            pl.BlockSpec((64, 1024), lambda i: (i, 0)),
            pl.BlockSpec((128, 256), lambda i: (i, 0)),
            pl.BlockSpec((1, 1024), lambda i: (0, 0)),
        ),
    )(passed.reshape(2, 256, 1024), qkv_grad, out_grad, gain_grad)
    return (passed[None], qkv_grad[None], out_grad[None], gain_grad)


def solution(mesh):
    placed = (
        P("section", "dp", None, "tensor"),
        P("section", None),
        P("section", "dp", None, "tensor"),
        P("section", "dp", None, "tensor"),
        P("section", "dp", None, "tensor"),
        P("section", "dp", None, "tensor"),
        P("section", None, "dp"),
        P("section", "dp", None),
        P("section", None, "tensor"),
        P("section", "tensor", None),
    )
    return jax.shard_map(
        shards,
        mesh=mesh,
        in_specs=placed,
        out_specs=(
            P("section", "dp", None, "tensor"),
            P("section", "dp", "tensor"),
            P("section", "tensor", "dp"),
            P("section", "tensor"),
        ),
        check_vma=False,
    )
```

```python
import math

import jax
import jax.numpy as jnp
from jax import lax
from jax.experimental import pallas as pl
from jax.experimental.pallas import tpu as pltpu
from jax.sharding import PartitionSpec as P

HD = 128
EPS = 1e-05
MESH = pl.DeviceIdType.MESH
F32 = jnp.float32
BF16 = jnp.bfloat16
SIX = ("fa", "fb", "rb", "la", "ra", "lb")
SCALE = 1.0 / math.sqrt(HD)

NT = (((1,), (1,)), ((), ()))
NN = (((1,), (0,)), ((), ()))
TN = (((0,), (0,)), ((), ()))


def dot(a, b, dims):
    return lax.dot_general(a, b, dims, preferred_element_type=F32)


def rows_of(index, size):
    return pl.ds(pl.multiple_of(index * size, size), size)


def as_row(column):
    return jnp.broadcast_to(column, (256, 128)).T[0:8, :]


def as_column(row):
    return jnp.broadcast_to(row, (128, 256)).T


def kernel(
    up_hbm, inp_hbm, q_hbm, k_hbm, v_hbm, seg, gain, order, wq_hbm, wo_hbm,
    passed, qg, og, gg,
    upb, nms, nmz, wo, wq, probs, ao, aga, wide, qk,
    o_s, o_y1, o_y2, o_x, o_x1, o_x2,
    q_y, q_y1, q_y2,
    g_1, g_2, ssq, rowp, root, rtot, segc, gp, gz, gy, gx,
    up_raw, inp_raw, q_raw, k_raw, v_raw, up, inp, q, k, v, un,
    lsem, ssem, rsem,
):
    sec = lax.axis_index("section")
    dp = lax.axis_index("dp")
    z = lax.axis_index("tensor")
    y = lax.div(dp, 4)
    x = lax.rem(dp, 4)

    z_to = [{"tensor": lax.rem(z + s, 4)} for s in range(4)]
    x_to = [{"dp": y * 4 + lax.rem(x + s, 4)} for s in range(4)]
    y_to = [{"dp": lax.rem(y + s, 4) * 4 + x} for s in range(4)]
    other = {"section": 1 - sec}

    counter = [0]
    sent = []

    def copy(src, dst, to, keep=True):
        index = counter[0]
        counter[0] += 1
        made = pltpu.make_async_remote_copy(
            src_ref=src,
            dst_ref=dst,
            send_sem=ssem.at[index],
            recv_sem=rsem.at[index],
            device_id=to,
            device_id_type=MESH,
        )
        if keep:
            sent.append(made)
        return made

    stored = ((up_hbm, up_raw, up), (inp_hbm, inp_raw, inp), (q_hbm, q_raw, q), (k_hbm, k_raw, k), (v_hbm, v_raw, v))
    fetches = [
        pltpu.make_async_copy(source, raw, lsem.at[5 + i]) for i, (source, raw, _) in enumerate(stored)
    ]
    loads = [
        pltpu.make_async_copy(wo_hbm.at[:, pl.ds(1024 * b, 1024)], wo.at[b], lsem.at[b])
        for b in range(4)
    ]
    loads.append(pltpu.make_async_copy(wq_hbm, wq, lsem.at[4]))
    for one in fetches + loads:
        one.start()

    def as_rows(which):
        fetches[which].wait()
        _, raw, kept = stored[which]

        @pl.loop(0, 16)
        def _(i):
            kept[rows_of(i, 32), :] = raw[rows_of(i, 16)].reshape(32, 1024)

    def by_micro(which):
        fetches[which].wait()
        _, raw, kept = stored[which]

        @pl.loop(0, 16)
        def _(i):
            for m in range(2):
                kept[pl.ds(pl.multiple_of(256 * m + i * 16, 16), 16), :] = raw[rows_of(i, 16), m, :]

    barrier = pltpu.get_barrier_semaphore()
    peers = z_to[1:] + x_to[1:] + y_to[1:] + [other]
    for peer in peers:
        pl.semaphore_signal(barrier, inc=1, device_id=peer, device_id_type=MESH)
    pl.semaphore_wait(barrier, len(peers))

    first, second = pl.ds(0, 256), pl.ds(256, 256)

    def gather(slots, to, a, b):
        own, right, far, left = slots
        return {
            "ra": copy(own.at[a], left.at[a], to[1]),
            "lb": copy(own.at[b], right.at[b], to[3]),
            "rb": copy(own.at[b], left.at[b], to[1]),
            "la": copy(own.at[a], right.at[a], to[3]),
            "fa": copy(left.at[a], far.at[a], to[1]),
            "fb": copy(right.at[b], far.at[b], to[3]),
        }

    def gather_start(made):
        for name in ("ra", "lb", "rb", "la"):
            made[name].start()

    def gather_relay(made):
        made["ra"].wait_recv()
        made["fa"].start()
        made["lb"].wait_recv()
        made["fb"].start()

    def gather_wait(made):
        for name in ("rb", "la", "fa", "fb"):
            made[name].wait_recv()

    def add_rows(dst, src, count, step=32):
        @pl.loop(0, count // step)
        def _(i):
            part = rows_of(i, step)
            dst[part, :] = (dst[part, :].astype(F32) + src[part, :].astype(F32)).astype(BF16)

    def scatter(far, right, left, half, land, full, to, keep=True):
        a, b = pl.ds(0, half), pl.ds(half, half)
        return {
            "fa": copy(far.at[a], land.at[0], to[1], keep),
            "fb": copy(far.at[b], land.at[1], to[3], keep),
            "rb": copy(right.at[b], full.at[0, b], to[1], keep),
            "la": copy(left.at[a], full.at[1, a], to[3], keep),
            "ra": copy(right.at[a], full.at[0, a], to[1], keep),
            "lb": copy(left.at[b], full.at[1, b], to[3], keep),
            "add_a": (right.at[a], land.at[0], half),
            "add_b": (left.at[b], land.at[1], half),
        }

    def scatter_start(made):
        for name in ("fa", "fb", "rb", "la"):
            made[name].start()

    def scatter_mid_a(made):
        made["fa"].wait_recv()
        add_rows(*made["add_a"])
        made["ra"].start()

    def scatter_mid_b(made):
        made["fb"].wait_recv()
        add_rows(*made["add_b"])
        made["lb"].start()

    def scatter_mid(made):
        scatter_mid_a(made)
        scatter_mid_b(made)

    def scatter_wait(made):
        for name in ("rb", "la", "ra", "lb"):
            made[name].wait_recv()

    up_slots = [up, upb.at[0], upb.at[1], upb.at[2]]
    up_made = gather(up_slots, z_to, first, second)
    as_rows(0)
    up_made["ra"].start()
    up_made["lb"].start()
    as_rows(1)

    for m in range(2):
        total = jnp.zeros((256, 1), F32)
        for c in range(4):
            part = inp[pl.ds(256 * m, 256), pl.ds(256 * c, 256)].astype(F32)
            total += jnp.sum(part * part, axis=-1, keepdims=True)
        ssq[0, :, pl.ds(256 * m, 256)] = as_row(total)
    ssq_made = [copy(ssq.at[0], ssq.at[s], z_to[s]) for s in (1, 2, 3)]
    for one in ssq_made:
        one.start()
    up_made["rb"].start()
    up_made["la"].start()
    for which in (2, 3, 4):
        by_micro(which)

    for m in range(2):
        ids = seg[pl.ds(m, 1), :].astype(F32)
        segc[pl.ds(256 * m, 256), :] = jnp.broadcast_to(ids, (256, 256)).T

    @pl.loop(0, 8)
    def _(i):
        m = lax.div(i, 4)
        head = lax.rem(i, 4)
        rows = rows_of(m, 256)
        lanes = rows_of(lax.div(head, 2), 128)
        scores = dot(q[rows, rows_of(head, 128)], k[rows, lanes], NT) * SCALE
        low = lax.broadcasted_iota(jnp.int32, (256, 256), 0)
        high = lax.broadcasted_iota(jnp.int32, (256, 256), 1)
        ids = seg[pl.ds(m, 1), :].astype(F32)
        visible = (segc[rows, :] == ids) & (high <= low)
        scores = jnp.where(visible, scores, -1e30)
        top = jnp.max(scores, axis=-1, keepdims=True)
        shifted = jnp.where(visible, jnp.exp(scores - top), 0.0)
        weights = shifted / jnp.sum(shifted, axis=-1, keepdims=True)
        probs[i] = weights
        wide[head, pl.ds(m, 256, stride=2), :] = dot(weights.astype(BF16), v[rows, lanes], NN)

    @pl.loop(0, 4)
    def _(i):
        ao[rows_of(i, 128), :] = wide[i].T.astype(BF16)

    for one in loads[:4]:
        one.wait()

    def take_upstream(slot):
        block = lax.rem(z + slot, 4)
        ref = up_slots[slot]

        @pl.loop(0, 2)
        def _(m):
            rows = rows_of(m, 256)
            term = dot(ref[rows, :], wo[block], NT)
            for c in range(4):
                part = term[:, 128 * c : 128 * c + 128]
                aga[c, rows, :] = part if slot == 0 else aga[c, rows, :] + part

    o_made = scatter(
        o_s.at[lax.rem(y + 2, 4)], o_s.at[lax.rem(y + 1, 4)], o_s.at[lax.rem(y + 3, 4)],
        256, o_y1, o_y2, y_to,
    )

    def out_terms(slot):
        block = lax.rem(z + slot, 4)
        ref = up_slots[slot]

        @pl.loop(0, 4)
        def _(j):
            lanes = rows_of(j, 256)
            o_s[block, :, lanes] = dot(ao[...], ref[:, lanes], NN).astype(BF16)

        role = lax.rem(block - y + 4, 4)

        @pl.when(role == 2)
        def _():
            o_made["fa"].start()
            o_made["fb"].start()

        @pl.when(role == 1)
        def _():
            o_made["rb"].start()

        @pl.when(role == 3)
        def _():
            o_made["la"].start()

    def out_mid(slot):
        role = lax.rem(lax.rem(z + slot, 4) - y + 4, 4)

        @pl.when(role == 1)
        def _():
            scatter_mid_a(o_made)

        @pl.when(role == 3)
        def _():
            scatter_mid_b(o_made)

    take_upstream(0)
    out_terms(0)
    gather_relay(up_made)

    for one in ssq_made:
        one.wait_recv()
    for m in range(2):
        lanes = pl.ds(256 * m, 256)
        total = ssq[0, :, lanes] + ssq[1, :, lanes] + ssq[2, :, lanes] + ssq[3, :, lanes]
        root[lanes, :] = as_column((1.0 / jnp.sqrt(total * (1.0 / 4096) + EPS))[0:1, :])

    for j in range(4):
        target = lax.rem(x + j, 4)
        lanes = rows_of(target, 256)
        part = gain[:, rows_of(z * 4 + target, 256)]
        kept = nmz.at[0, 0] if j == 0 else nms.at[j - 1]

        @pl.loop(0, 4)
        def _(i):
            rows = rows_of(i, 128)
            unit = inp[rows, lanes].astype(F32) * root[rows, 0:1]
            un[rows, lanes] = unit
            kept[:, rows] = (unit * part).T.astype(BF16)

    nx_made = [copy(nms.at[j - 1], nmz.at[0, 4 - j], x_to[j]) for j in (1, 2, 3)]
    for one in nx_made:
        one.start()

    up_made["rb"].wait_recv()
    take_upstream(3)
    out_terms(3)
    up_made["la"].wait_recv()
    take_upstream(1)
    out_terms(1)

    for one in nx_made:
        one.wait_recv()
    nm_made = gather([nmz.at[r] for r in range(4)], z_to, pl.ds(0, 2), pl.ds(2, 2))
    gather_start(nm_made)

    up_made["fa"].wait_recv()
    up_made["fb"].wait_recv()
    take_upstream(2)

    out_mid(0)

    qk_made = [
        gather([qk.at[group, r] for r in range(4)], x_to, first, second) for group in range(2)
    ]
    for group in range(2):
        lanes = pl.ds(128 * group, 128)

        @pl.loop(0, 2)
        def _(m):
            rows = rows_of(m, 256)
            mine = pl.ds(m, 256, stride=2)
            key_grad = jnp.zeros((256, 128), F32)
            value_grad = jnp.zeros((256, 128), F32)
            for h in range(2):
                head = pl.ds(128 * (group * 2 + h), 128)
                grad = aga[group * 2 + h, mine, :].astype(BF16)
                weights = probs[m * 4 + group * 2 + h]
                probs_grad = dot(grad, v[rows, lanes], NT)
                row_dot = jnp.sum(weights * probs_grad, axis=-1, keepdims=True)
                score_grad = (weights * (probs_grad - row_dot) * SCALE).astype(BF16)
                wide[h, mine, :] = dot(score_grad, k[rows, lanes], NN)
                key_grad += dot(score_grad, q[rows, head], TN)
                value_grad += dot(weights.astype(BF16), grad, TN)
            wide[2, mine, :] = key_grad
            wide[3, mine, :] = value_grad

        @pl.loop(0, 8)
        def _(i):
            rows = rows_of(i, 64)
            for c in range(4):
                qk[group, 0, rows, pl.ds(128 * c, 128)] = wide[c, rows, :].astype(BF16)

        if group == 0:
            gather_start(qk_made[0])

    out_terms(2)
    out_mid(3)
    out_mid(1)
    gather_relay(qk_made[0])
    gather_start(qk_made[1])
    gather_relay(nm_made)
    loads[4].wait()

    q_made = [
        scatter(
            q_y.at[group, lax.rem(y + 2, 4)], q_y.at[group, lax.rem(y + 1, 4)],
            q_y.at[group, lax.rem(y + 3, 4)], 128, q_y1.at[group], q_y2.at[group], y_to,
        )
        for group in range(2)
    ]

    def qkv_terms(group, slot):
        block = lax.rem(z + slot, 4)
        role = lax.rem(block - y + 4, 4)
        made = q_made[group]
        normed = jnp.concatenate([nmz[slot, r] for r in range(4)], axis=1)
        term = dot(normed, qk[group].reshape(2048, 512), NN)
        q_y[group, block] = term.astype(BF16)

        @pl.when(role == 2)
        def _():
            made["fa"].start()
            made["fb"].start()

        @pl.when(role == 1)
        def _():
            made["rb"].start()

        @pl.when(role == 3)
        def _():
            made["la"].start()

        weight = wq[block, rows_of(x, 256), pl.ds(512 * group, 512)].astype(F32)
        row = as_row(jnp.sum(term * weight, axis=-1, keepdims=True))
        if group == 0:
            gp[slot] = row
        else:
            gp[slot] += row

    def qkv_mid(group, slot):
        role = lax.rem(lax.rem(z + slot, 4) - y + 4, 4)

        @pl.when(role == 1)
        def _():
            scatter_mid_a(q_made[group])

        @pl.when(role == 3)
        def _():
            scatter_mid_b(q_made[group])

    z_made = scatter(wo.at[2], wo.at[1], wo.at[3], 256, g_1, g_2, z_to, keep=False)

    @pl.when(sec == 1)
    def _():
        @pl.loop(0, 16)
        def _(i):
            j = lax.div(i, 4)
            part = rows_of(lax.rem(i, 4), 256)
            at = lax.rem(z + j, 4)
            term = dot(qk[0, 0], wq[at, part, pl.ds(0, 512)], NT)
            term += dot(qk[1, 0], wq[at, part, pl.ds(512, 512)], NT)
            wo[j, :, part] = term.astype(BF16)

        scatter_start(z_made)

    gather_wait(qk_made[0])
    qkv_terms(0, 0)
    nm_made["rb"].wait_recv()
    qkv_terms(0, 3)
    nm_made["la"].wait_recv()
    qkv_terms(0, 1)
    out_mid(2)
    gather_relay(qk_made[1])
    qkv_mid(0, 0)
    nm_made["fa"].wait_recv()
    nm_made["fb"].wait_recv()
    qkv_terms(0, 2)
    qkv_mid(0, 3)
    qkv_mid(0, 1)

    @pl.when(sec == 1)
    def _():
        scatter_mid(z_made)

    gather_wait(qk_made[1])
    for slot in (0, 3, 1, 2):
        qkv_terms(1, slot)

    qkv_mid(0, 2)

    gz_made = [copy(gp.at[r], gz.at[r - 1], z_to[r]) for r in (1, 2, 3)]
    for one in gz_made:
        one.start()

    scatter_wait(o_made)
    o_own = o_s.at[y]

    @pl.loop(0, 4)
    def _(j):
        lanes = rows_of(lax.rem(x + j, 4), 256)

        @pl.loop(0, 8)
        def _(i):
            rows = rows_of(i, 64)
            total = (
                o_own[rows, lanes].astype(F32)
                + o_y2[0, rows, lanes].astype(F32)
                + o_y2[1, rows, lanes].astype(F32)
            )
            o_x[j, rows, :] = total.astype(BF16)

    ox_made = scatter(o_x.at[2], o_x.at[1], o_x.at[3], 256, o_x1, o_x2, x_to)
    scatter_start(ox_made)
    qkv_mid(1, 0)
    qkv_mid(1, 3)
    qkv_mid(1, 1)

    for one in gz_made:
        one.wait_recv()
    gy[0] = gp[0] + gz[0] + gz[1] + gz[2]
    gy_made = [copy(gy.at[0], gy.at[s], y_to[s]) for s in (1, 2, 3)]
    for one in gy_made:
        one.start()

    layer = upb.at[1]
    row_made = [copy(rowp.at[0], rowp.at[s], z_to[s], keep=False) for s in (1, 2, 3)]

    def scaled_unit(rows):
        grad = (
            wo[0, rows, :].astype(F32) + g_2[0, rows, :].astype(F32) + g_2[1, rows, :].astype(F32)
        )
        return grad * gain[:, rows_of(z, 1024)], un[rows, :]

    @pl.when(sec == 1)
    def _():
        scatter_wait(z_made)

        @pl.loop(0, 16)
        def _(i):
            rows = rows_of(i, 32)
            scaled, unit = scaled_unit(rows)
            part = jnp.sum(scaled * unit, axis=-1, keepdims=True)
            rtot[rows, :] = jnp.broadcast_to(part, (32, 128))

        for m in range(2):
            lanes = pl.ds(256 * m, 256)
            rowp[0, :, lanes] = rtot[lanes, :].T[0:8, :]
        for one in row_made:
            one.start()

    qkv_mid(1, 2)
    scatter_mid(ox_made)

    for one in gy_made:
        one.wait_recv()
    gx[x] = (gy[0] + gy[1] + gy[2] + gy[3]) / (gain[:, rows_of(z * 4 + x, 256)] * 16.0)
    gx_made = [copy(gx.at[x], gx.at[x], x_to[s]) for s in (1, 2, 3)]
    for one in gx_made:
        one.start()

    pieces = [pl.ds(128 * i, 128) for i in range(4)]
    passed_made = [copy(layer.at[piece], passed.at[piece], other, keep=False) for piece in pieces]

    @pl.when(sec == 1)
    def _():
        for one in row_made:
            one.wait_recv()
        for m in range(2):
            lanes = pl.ds(256 * m, 256)
            total = rowp[0, :, lanes] + rowp[1, :, lanes] + rowp[2, :, lanes] + rowp[3, :, lanes]
            rtot[lanes, :] = as_column((total * (1.0 / 4096))[0:1, :])
        straight = order[0:1, 0:1] == 0

        even = lax.rem(lax.broadcasted_iota(jnp.int32, (4, 8, 1024), 1), 2) == 0
        keep_order = jnp.broadcast_to(straight, (4, 8, 1024))
        for piece in range(4):

            @pl.loop(4 * piece, 4 * piece + 4)
            def _(i):
                rows = rows_of(i, 32)
                scaled, unit = scaled_unit(rows)
                through = up[rows, :].astype(F32) + (scaled - unit * rtot[rows, 0:1]) * root[rows, 0:1]
                through = through.reshape(4, 8, 1024)
                swapped = jnp.where(even, pltpu.roll(through, 7, 1), pltpu.roll(through, 1, 1))
                picked = jnp.where(keep_order, through, swapped)
                layer[rows, :] = picked.reshape(32, 1024).astype(BF16)

            passed_made[piece].start()

        @pl.loop(0, 16)
        def _(i):
            passed[rows_of(i, 32), :] = jnp.zeros((32, 1024), BF16)

    scatter_wait(ox_made)

    @pl.loop(0, 8)
    def _(i):
        rows = rows_of(i, 64)
        total = o_x[0, rows, :].astype(F32) + o_x2[0, rows, :].astype(F32) + o_x2[1, rows, :].astype(F32)
        og[rows, :] = total * (1.0 / 16)

    for one in gx_made:
        one.wait_recv()
    for s in range(4):
        gg[:, pl.ds(256 * s, 256)] = gx[s]

    for group in range(2):
        scatter_wait(q_made[group])

        @pl.loop(0, 4)
        def _(i):
            rows = rows_of(i, 64)
            total = (
                q_y[group, y, rows, :].astype(F32)
                + q_y2[group, 0, rows, :].astype(F32)
                + q_y2[group, 1, rows, :].astype(F32)
            )
            qg[rows, pl.ds(512 * group, 512)] = total * (1.0 / 16)

    @pl.when(sec == 0)
    def _():
        for one in passed_made:
            one.wait_recv()

    @pl.when(sec == 1)
    def _():
        for one in [z_made[name] for name in SIX] + row_made + passed_made:
            one.wait_send()

    for one in sent:
        one.wait_send()


def finish(passed, qkv_sum, out_sum, gain_sum, passed_out, qkv_out, out_out, gain_out):
    passed_out[...] = passed[...].reshape(64, 2, 1024)
    qkv_out[...] = qkv_sum[...]
    out_out[...] = out_sum[...]
    gain_out[...] = gain_sum[0:1, :]


def shards(
    layer_input,
    norm_gain,
    upstream_grad,
    saved_queries,
    saved_keys,
    saved_values,
    segment_ids,
    batch_order,
    qkv_weight,
    out_weight,
):
    vmem = pl.BlockSpec(memory_space=pltpu.VMEM)
    hbm = pl.BlockSpec(memory_space=pl.ANY)
    passed, qkv_grad, out_grad, gain_grad = pl.pallas_call(
        kernel,
        out_shape=(
            jax.ShapeDtypeStruct((512, 1024), BF16),
            jax.ShapeDtypeStruct((256, 1024), F32),
            jax.ShapeDtypeStruct((512, 256), F32),
            jax.ShapeDtypeStruct((8, 1024), F32),
        ),
        in_specs=[hbm] * 5 + [vmem] * 3 + [hbm] * 2,
        out_specs=(vmem,) * 4,
        scratch_shapes=[
            pltpu.VMEM((3, 512, 1024), BF16),
            pltpu.VMEM((3, 256, 512), BF16),
            pltpu.VMEM((4, 4, 256, 512), BF16),
            pltpu.VMEM((4, 512, 1024), BF16),
            pltpu.VMEM((4, 1024, 1024), BF16),
            pltpu.VMEM((8, 256, 256), F32),
            pltpu.VMEM((512, 512), BF16),
            pltpu.VMEM((4, 512, 128), F32),
            pltpu.VMEM((4, 512, 128), F32),
            pltpu.VMEM((2, 4, 512, 512), BF16),
            pltpu.VMEM((4, 512, 1024), BF16),
            pltpu.VMEM((2, 256, 1024), BF16),
            pltpu.VMEM((2, 512, 1024), BF16),
            pltpu.VMEM((4, 512, 256), BF16),
            pltpu.VMEM((2, 256, 256), BF16),
            pltpu.VMEM((2, 512, 256), BF16),
            pltpu.VMEM((2, 4, 256, 512), BF16),
            pltpu.VMEM((2, 2, 128, 512), BF16),
            pltpu.VMEM((2, 2, 256, 512), BF16),
            pltpu.VMEM((2, 256, 1024), BF16),
            pltpu.VMEM((2, 512, 1024), BF16),
            pltpu.VMEM((4, 8, 512), F32),
            pltpu.VMEM((4, 8, 512), F32),
            pltpu.VMEM((512, 128), F32),
            pltpu.VMEM((512, 128), F32),
            pltpu.VMEM((512, 256), F32),
            pltpu.VMEM((4, 8, 256), F32),
            pltpu.VMEM((3, 8, 256), F32),
            pltpu.VMEM((4, 8, 256), F32),
            pltpu.VMEM((4, 8, 256), F32),
            pltpu.VMEM((256, 2, 1024), BF16),
            pltpu.VMEM((256, 2, 1024), BF16),
            pltpu.VMEM((256, 2, 512), BF16),
            pltpu.VMEM((256, 2, 256), BF16),
            pltpu.VMEM((256, 2, 256), BF16),
            pltpu.VMEM((512, 1024), BF16),
            pltpu.VMEM((512, 1024), BF16),
            pltpu.VMEM((512, 512), BF16),
            pltpu.VMEM((512, 256), BF16),
            pltpu.VMEM((512, 256), BF16),
            pltpu.VMEM((512, 1024), F32),
            pltpu.SemaphoreType.DMA((10,)),
            pltpu.SemaphoreType.DMA((90,)),
            pltpu.SemaphoreType.DMA((90,)),
        ],
        compiler_params=pltpu.CompilerParams(
            collective_id=0, has_side_effects=True, vmem_limit_bytes=67043328
        ),
    )(
        upstream_grad[0],
        layer_input[0],
        saved_queries[0],
        saved_keys[0],
        saved_values[0],
        segment_ids[0],
        norm_gain,
        batch_order[0],
        qkv_weight[0].reshape(4, 1024, 1024),
        out_weight[0],
    )
    passed, qkv_grad, out_grad, gain_grad = pl.pallas_call(
        finish,
        grid=(4,),
        out_shape=(
            jax.ShapeDtypeStruct((256, 2, 1024), BF16),
            jax.ShapeDtypeStruct((256, 1024), F32),
            jax.ShapeDtypeStruct((512, 256), F32),
            jax.ShapeDtypeStruct((1, 1024), F32),
        ),
        in_specs=[
            pl.BlockSpec((128, 1024), lambda i: (i, 0)),
            pl.BlockSpec((64, 1024), lambda i: (i, 0)),
            pl.BlockSpec((128, 256), lambda i: (i, 0)),
            pl.BlockSpec((8, 1024), lambda i: (0, 0)),
        ],
        out_specs=(
            pl.BlockSpec((64, 2, 1024), lambda i: (i, 0, 0)),
            pl.BlockSpec((64, 1024), lambda i: (i, 0)),
            pl.BlockSpec((128, 256), lambda i: (i, 0)),
            pl.BlockSpec((1, 1024), lambda i: (0, 0)),
        ),
    )(passed, qkv_grad, out_grad, gain_grad)
    return (passed[None], qkv_grad[None], out_grad[None], gain_grad)


def solution(mesh):
    placed = (
        P("section", "dp", None, "tensor"),
        P("section", None),
        P("section", "dp", None, "tensor"),
        P("section", "dp", None, "tensor"),
        P("section", "dp", None, "tensor"),
        P("section", "dp", None, "tensor"),
        P("section", None, "dp"),
        P("section", "dp", None),
        P("section", None, "tensor"),
        P("section", "tensor", None),
    )
    return jax.shard_map(
        shards,
        mesh=mesh,
        in_specs=placed,
        out_specs=(
            P("section", "dp", None, "tensor"),
            P("section", "dp", "tensor"),
            P("section", "tensor", "dp"),
            P("section", "tensor"),
        ),
        check_vma=False,
    )
```
